32 devices in a mesh: station: 4 (over z), group: 4 (over x, core), bias: 2 (over y).
Axes of the slice: x: 2, y: 2, z: 4, core: 2. Of those that a mesh axis runs over, the one named last changes fastest.
Arguments:
- normal_mat: float32 [128, 2304], P(('station', 'group')), may hold values from -16 to 18, as said below
- coupling: float32 [128, 2, 8, 48, 128], P(('station', 'group'), 'bias'), may hold values from -0.13258252 to 0.13258252
- lengths: int32 [128], P(('station', 'group')), may hold values from 12 to 48
- visible: int32 [128, 2, 8], P(('station', 'group'), 'bias'), may hold values from 0 to 16, as said below
- bias_prior: float32 [2, 16, 128], P('bias', 'station'), may hold values from 0.1 to 1
- unimod: int32 [128, 2304], P(('station', 'group')), may hold values from -1 to 2, as said below
Outputs:
- bias_cov: float32 [2, 16, 128, 128], P('bias', 'station')
- amb_cov: float32 [128, 2304], P(('station', 'group'))
The draws below stay inside these ranges and needn't reach their ends.
Inputs may be any that keep to these rules, and one draw needn't show every extreme that they name: `normal_mat`: each station's matrix, read as 48 x 48 row by row, is symmetric with all eigenvalues 1 or more. Each list visible[s, h] holds distinct block numbers below 16 in its first slots and the value 16 in its unused slots; every list has at least one block; in every draw the stations of some devices use all 8 slots. `unimod`: each station's matrix, read as 48 x 48 row by row, is a unit lower triangular times a unit upper triangular integer matrix; each row of the lower factor and each column of the upper factor holds at most one entry off the diagonal, -1 or 1; so every leading square block has determinant 1.
All inputs are finite; a program needn't handle non-finite values.
Results may differ from the reference program's by a relative error of at most 0.0003.
Values sent between devices are 32-bit elements; how exact they have to be, the bound alone decides.
No kernel may reach another device: no remote copies, remote signals or barrier semaphores. Data moves between devices by JAX's collectives and lax.ppermute only.
A program may use at most 64 MiB of HBM per device.

```python
import math
import jax
import jax.numpy as jnp
from jax import lax

A = 48
BS = 128
VH = 8
S_DEV = 8
NHALF = 16
STATIONS = 128


def draw_normal_mat(key, part):
    first_key = jax.random.fold_in(jax.random.fold_in(key, 11), 0)
    base = jnp.clip(jax.random.normal(first_key, (STATIONS, A, A), jnp.float32), -4.0, 4.0)
    lift = jax.random.uniform(jax.random.fold_in(key, 12), (STATIONS, A), jnp.float32, 0.0, 1.0)
    light_mean = (1 + VH // 2) / 2.0
    per_half = 0.25 * VH + 0.75 * light_mean
    per_block = STATIONS * per_half / NHALF
    mean_len = (A // 4 + A) / 2.0
    coupling_var = 1.0 / (2.0 * BS * VH)
    target = min(0.5, 0.9 / (per_block * mean_len * coupling_var))
    strength = target / (1.5 * (1.0 - target))
    gram = jnp.einsum('sab,scb->sac', base, base, precision=lax.Precision.HIGHEST) / A
    matrix = strength * (gram + lift[:, :, None] * jnp.eye(A, dtype=jnp.float32)) + jnp.eye(A, dtype=jnp.float32)
    return matrix.reshape(STATIONS, A * A)


def draw_visible(key, part):
    keys = jax.random.split(jax.random.fold_in(key, 21), 4)
    owners = STATIONS // S_DEV
    heavy = (jax.random.randint(keys[0], (owners,), 0, 4) == 0) | (jnp.arange(owners, dtype=jnp.int32) == jax.random.randint(keys[3], (), 0, owners))
    heavy = jnp.repeat(heavy, S_DEV)
    light = jax.random.randint(keys[1], (STATIONS, 2), 1, VH // 2 + 1)
    filled = jnp.where(heavy[:, None], VH, light)
    scores = jax.random.randint(keys[2], (STATIONS, 2, NHALF), 0, 65536) * NHALF + jnp.arange(NHALF, dtype=jnp.int32)
    ordered = jnp.argsort(scores, axis=-1)[..., :VH].astype(jnp.int32)
    slots = jnp.arange(VH, dtype=jnp.int32)
    return jnp.where(slots < filled[..., None], ordered, NHALF).astype(jnp.int32)


def factor_entries(pick_key, sign_key, live_key, positions):
    reach = jnp.maximum(positions, 1)
    picked = jax.random.randint(pick_key, (STATIONS, A), 0, 1 << 20) % reach
    signs = 2 * jax.random.randint(sign_key, (STATIONS, A), 0, 2) - 1
    live = jax.random.randint(live_key, (STATIONS, A), 0, 2) * (positions >= 1).astype(jnp.int32)
    return (picked.astype(jnp.int32), (signs * live).astype(jnp.int32))


def draw_unimod(key, part):
    keys = jax.random.split(jax.random.fold_in(key, 31), 6)
    positions = jnp.arange(A, dtype=jnp.int32)
    lower_pick, lower_value = factor_entries(keys[0], keys[1], keys[2], positions)
    upper_pick, upper_value = factor_entries(keys[3], keys[4], keys[5], positions)
    first = jnp.arange(STATIONS, dtype=jnp.int32)[:, None] == 0
    lower_value = jnp.where(first & (positions == 1), 1, lower_value)
    lower_value = jnp.where(first & (positions == 2), -1, lower_value)
    lower_pick = jnp.where(first & (positions == 2), 0, lower_pick)
    upper_value = jnp.where(first & (positions == 1), 1, upper_value)
    identity = jnp.eye(A, dtype=jnp.int32)
    lower = identity + lower_value[:, :, None] * (lower_pick[:, :, None] == positions).astype(jnp.int32)
    upper = identity + upper_value[:, None, :] * (upper_pick[:, None, :] == positions[:, None]).astype(jnp.int32)
    product = jnp.einsum('sab,sbc->sac', lower, upper)
    return product.reshape(STATIONS, A * A).astype(jnp.int32)


def place_ends(entries, key, low, high):
    spot = [jax.random.randint(jax.random.fold_in(key, axis), (), 0, length) for axis, length in enumerate(entries.shape)]
    widest = entries.shape.index(max(entries.shape))
    next_to = spot[:widest] + [(spot[widest] + 1) % entries.shape[widest]] + spot[widest + 1:]
    return entries.at[tuple(spot)].set(low).at[tuple(next_to)].set(high)


def shard_levels(stream_key, dims, cuts, low, top_value):
    level, own = 1.0, jax.random.fold_in(stream_key, 6)
    for axis_at, shards_of in cuts:
        heights = jnp.exp(jax.random.uniform(jax.random.fold_in(own, axis_at), (shards_of,), jnp.float32, low / len(cuts), top_value / len(cuts)))
        level = level * jnp.repeat(heights, dims[axis_at] // shards_of).reshape([-1 if axis == axis_at else 1 for axis in range(len(dims))])
    return level


def bell_draw(own_key, shape, width, bound, cuts=(), held_as=jnp.bfloat16):
    gain = shard_levels(own_key, shape, cuts, -0.22, 0.18) if cuts else 1.0
    result = jax.random.normal(own_key, shape, jnp.float32) * width * gain
    return jnp.minimum(jnp.maximum(result, -bound), bound).astype(held_as)


def setup_inputs(seed: int = 0) -> dict:
    key_of = jax.random.split(jax.random.key(seed), 7)
    normal_mat = draw_normal_mat(jax.random.fold_in(key_of[6], 71), 0)
    coupling = bell_draw(key_of[1], (STATIONS, 2, VH, A, BS), ((2 * BS * VH) ** -0.5), 0.13258252, ((0, 16), (1, 2)), jnp.float32)
    lengths = place_ends(jax.random.randint(key_of[2], (STATIONS,), A // 4, A + 1), jax.random.fold_in(key_of[2], 1), A // 4, A).astype(jnp.int32)
    visible = draw_visible(jax.random.fold_in(key_of[6], 71), 0)
    bias_prior = jnp.clip(jnp.exp(math.log(1.0) - 2.3025851 * jax.random.uniform(key_of[4], (2, NHALF, BS), jnp.float32) ** shard_levels(key_of[4], (2, NHALF, BS), ((0, 2), (1, 4)), -0.2, 0.2)), 0.1, 1.0)
    unimod = draw_unimod(jax.random.fold_in(key_of[6], 71), 0)
    return {"normal_mat": normal_mat, "coupling": coupling, "lengths": lengths, "visible": visible, "bias_prior": bias_prior, "unimod": unimod}


precise = lax.Precision.HIGHEST

def spd_inverse(matrix):
    matrix_order = matrix.shape[-1]
    factor = jnp.linalg.cholesky(matrix)
    identity = jnp.broadcast_to(jnp.eye(matrix_order, dtype=matrix.dtype), matrix.shape)
    lower_inv = lax.linalg.triangular_solve(factor, identity, left_side=True, lower=True)
    return jnp.einsum('...ka,...kb->...ab', lower_inv, lower_inv, precision=precise)

def prepare(normal_mat, coupling, lengths):
    stations = coupling.shape[0]
    block_len = coupling.shape[3]
    positions = jnp.arange(block_len, dtype=jnp.int32)
    row_valid = (positions[None, :] < lengths[:, None]).astype(jnp.float32)
    keep_mask = row_valid[:, :, None] * row_valid[:, None, :]
    stacked = normal_mat.reshape(stations, block_len, block_len)
    effective = keep_mask * stacked + (1.0 - keep_mask) * jnp.eye(block_len, dtype=jnp.float32)
    inverse = spd_inverse(effective)
    weighted = coupling * row_valid[:, None, None, :, None]
    solved = jnp.einsum('sab,shjbc->shjac', inverse, weighted, precision=precise)
    return (keep_mask, inverse, weighted, solved)

def reduced_terms(weighted, solved):
    return jnp.einsum('shjac,shjad->shjcd', weighted, weighted - solved, precision=precise)

def bias_share(solved, chosen):
    lifted = jnp.einsum('shjac,shjcd->shjad', solved, chosen, precision=precise)
    return jnp.einsum('shjad,shjbd->sab', lifted, solved, precision=precise)

def finish_cov(keep_mask, inverse, bias_part, unimod):
    stations = keep_mask.shape[0]
    block_len = keep_mask.shape[1]
    covariance = keep_mask * (inverse + bias_part)
    integer_map = unimod.reshape(stations, block_len, block_len).astype(jnp.float32)
    mapped = jnp.einsum('sab,sbc,sdc->sad', integer_map, covariance, integer_map, precision=precise)
    return (keep_mask * mapped).reshape(stations, block_len * block_len)

def reference(normal_mat, coupling, lengths, visible, bias_prior, unimod):
    stations = coupling.shape[0]
    block_width = coupling.shape[4]
    group_rows = math.gcd(stations, 64)
    block_count = stations // group_rows

    def split_rows(array):
        return array.reshape((block_count, group_rows) + array.shape[1:])
    columns = jnp.arange(NHALF, dtype=jnp.int32)

    def accumulate(running, pieces):
        normal_blk, couple_blk, length_blk, visible_blk = pieces
        keep_mask, inverse, weighted, solved = prepare(normal_blk, couple_blk, length_blk)
        selector = (visible_blk[..., None] == columns).astype(jnp.float32)
        reduced = reduced_terms(weighted, solved)
        return (running + jnp.einsum('shjx,shjcd->hxcd', selector, reduced, precision=precise), None)
    empty_table = jnp.zeros((2, NHALF, block_width, block_width), jnp.float32)
    block_table = lax.scan(accumulate, empty_table, (split_rows(normal_mat), split_rows(coupling), split_rows(lengths), split_rows(visible)))[0]
    bias_cov = spd_inverse(block_table + bias_prior[..., :, None] * jnp.eye(block_width, dtype=jnp.float32))

    def finish_block(pieces):
        normal_blk, couple_blk, length_blk, visible_blk, unimod_blk = pieces
        keep_mask, inverse, weighted, solved = prepare(normal_blk, couple_blk, length_blk)
        selector = (visible_blk[..., None] == columns).astype(jnp.float32)
        chosen = jnp.einsum('shjx,hxcd->shjcd', selector, bias_cov, precision=precise)
        return finish_cov(keep_mask, inverse, bias_share(solved, chosen), unimod_blk)
    amb_cov = lax.map(finish_block, (split_rows(normal_mat), split_rows(coupling), split_rows(lengths), split_rows(visible), split_rows(unimod)))
    return (bias_cov, amb_cov.reshape(stations, -1))
```

```python
import functools

import jax
import jax.numpy as jnp
from jax import lax
from jax.experimental import pallas as pl
from jax.experimental.pallas import tpu as pltpu
from jax.sharding import PartitionSpec as P

NHALF = 16
LANES = 128
SUB = 8
PANEL = 8
f32 = jnp.float32
bf16 = jnp.bfloat16


def bits_of(n):
    count = n.bit_length() - 1
    assert 1 << count == n
    return count


class Plan:
    def __init__(self, stations, groups):
        per = max(NHALF // stations, 1)
        own = min(bits_of(per), bits_of(groups))
        steps = [("group", g, bits_of(per) - 1 - g) for g in range(own)]
        steps += [("station", z, bits_of(per) + z) for z in range(bits_of(stations))]
        self.per = per
        self.sizes = {"station": stations, "group": groups}
        self.steps = steps
        self.sums = [("group", g) for g in range(own, bits_of(groups))]
        used = [b for _, _, b in steps]
        rest = [b for b in range(bits_of(NHALF)) if b not in used]
        top = bits_of(NHALF) - 1
        self.moves = [(top - t, b) for t, b in enumerate(used)]
        self.moves += list(zip(range(len(rest)), sorted(rest)))
        self.left = NHALF >> len(steps)

    def mask(self):
        out = 0
        for axis, bit, block_bit in self.steps:
            out = out + (((lax.axis_index(axis) >> bit) & 1) << block_bit)
        return out

    def position(self, block, mask):
        y = block ^ mask
        out = 0
        for p, b in self.moves:
            out = out + (((y >> b) & 1) << p)
        return out

    def block(self, position, mask):
        out = 0
        for p, b in self.moves:
            out = out + (((position >> p) & 1) << b)
        return out ^ mask

    def perm(self, axis, bit):
        return [(i, i ^ (1 << bit)) for i in range(self.sizes[axis])]


def split(x):
    hi = x.astype(bf16)
    return hi, (x - hi.astype(f32)).astype(bf16)


def dot3(a, b, dims):
    def d(x, y):
        return lax.dot_general(x, y, (dims, ((), ())), preferred_element_type=f32)

    return d(a[0], b[0]) + (d(a[0], b[1]) + d(a[1], b[0]))


NN = ((1,), (0,))
NT = ((1,), (1,))


def pick(x, idx):
    return jnp.take_along_axis(x, idx, axis=1)


def eliminate(rows, base, lane):
    b = len(rows)
    idx = [jnp.zeros((SUB, LANES), jnp.int32) + (base + j) for j in range(b)]
    p = [[pick(rows[i], idx[j]) for j in range(i + 1)] for i in range(b)]
    inside = (lane >= base) & (lane < base + b)
    y = [jnp.where(inside, (lane == base + i).astype(f32), rows[i]) for i in range(b)]
    l = [[None] * b for _ in range(b)]
    r = [None] * b
    for j in range(b):
        r[j] = 1.0 / p[j][j]
        for i in range(j + 1, b):
            l[i][j] = p[i][j] * r[j]
        for i in range(j + 1, b):
            for m in range(j + 1, i + 1):
                p[i][m] = p[i][m] - l[i][j] * p[m][j]
        for i in range(j + 1, b):
            y[i] = y[i] - l[i][j] * y[j]
    out = [None] * b
    for i in range(b - 1, -1, -1):
        t = y[i] * r[i]
        for j in range(b - 1, i, -1):
            t = t - l[j][i] * out[j]
        out[i] = t
    return out, idx, inside


def row_of(ref, i, n):
    at = i * n
    tile, off = at // LANES, at % LANES
    x = ref[:, tile * LANES:(tile + 1) * LANES]
    if off:
        x = pltpu.roll(x, LANES - off, 1)
        if off + n > LANES:
            nxt = ref[:, (tile + 1) * LANES:(tile + 2) * LANES]
            nxt = pltpu.roll(nxt, LANES - off, 1)
            lane = lax.broadcasted_iota(jnp.int32, (SUB, LANES), 1)
            x = jnp.where(lane < LANES - off, x, nxt)
    return x


def lengths_column(len_ref, stations):
    sub = lax.broadcasted_iota(jnp.int32, (SUB, LANES), 0)
    out = jnp.zeros((SUB, LANES), jnp.int32)
    for s in range(stations):
        out = jnp.where(sub == s, len_ref[s], out)
    return out


def first_kernel(plan, dims, len_ref, vis_ref, mat_ref, cpl_ref, inv_ref, sol_ref, *rest):
    stations, slots, n, width = dims
    outs, (rows_ref, acc_ref) = rest[:-2], rest[-2:]
    lane = lax.broadcasted_iota(jnp.int32, (SUB, LANES), 1)
    length = lengths_column(len_ref, stations)
    for i in range(n):
        x = row_of(mat_ref, i, n)
        keep = (lane < length) & (length > i)
        rows_ref[i] = jnp.where(keep, x, (lane == i).astype(f32))

    def step(k, c):
        base = k * PANEL
        out, idx, inside = eliminate([rows_ref[base + i] for i in range(PANEL)], base, lane)
        for v in range(n):
            a = rows_ref[v]
            t = jnp.where(inside, 0.0, a)
            for j in range(PANEL):
                t = t - pick(a, idx[j]) * out[j]
            rows_ref[v] = t
        for i in range(PANEL):
            rows_ref[base + i] = out[i]
        return c

    lax.fori_loop(0, n // PANEL, step, 0)
    for i in range(n):
        inv_ref[pl.ds(i, stations, stride=n), :] = rows_ref[i]
    acc_ref[...] = jnp.zeros_like(acc_ref)
    mask = plan.mask()
    tall = lax.broadcasted_iota(jnp.int32, (n, width), 0)

    def station(s, c):
        inverse = split(inv_ref[pl.ds(pl.multiple_of(s * n, SUB), n), :n])
        valid = tall < len_ref[s]
        for j in range(slots):
            w = jnp.where(valid, cpl_ref[s, j], 0.0)
            x = dot3(inverse, split(w), NN)
            sol_ref[s, j] = x
            red = dot3(split(w.T), split(w - x), NN)
            v = vis_ref[s, j]
            at = jnp.where(v < NHALF, plan.position(v, mask), NHALF)
            acc_ref[at] += red
        return c

    lax.fori_loop(0, stations, station, 0)
    at = NHALF
    for o in outs:
        at -= o.shape[0]
        o[...] = acc_ref[at:at + o.shape[0]]


def invert_kernel(plan, prior_ref, a_ref, b_ref, o_ref):
    lane = lax.broadcasted_iota(jnp.int32, (SUB, LANES), 1)
    sub = lax.broadcasted_iota(jnp.int32, (SUB, LANES), 0)
    nb, n, _ = o_ref.shape
    mask = plan.mask()
    first = lax.axis_index("station") * plan.per
    for q in range(nb):
        prior = prior_ref[pl.ds(plan.block(q, mask) - first, 1), :]
        prior = jnp.broadcast_to(prior, (SUB, n))
        for v in range(n // SUB):
            at = slice(SUB * v, SUB * v + SUB)
            diag = jnp.where(lane == sub + SUB * v, prior, 0.0)
            o_ref[q, at, :] = a_ref[q, at, :] + b_ref[q, at, :] + diag

    def step(k, c):
        base = k * PANEL
        for q in range(nb):
            rows = [jnp.broadcast_to(o_ref[q, pl.ds(base + i, 1), :], (SUB, LANES)) for i in range(PANEL)]
            out, idx, inside = eliminate(rows, base, lane)
            for v in range(n // SUB):
                at = slice(SUB * v, SUB * v + SUB)
                a = o_ref[q, at, :]
                t = jnp.where(inside, 0.0, a)
                for j in range(PANEL):
                    t = t - pick(a, idx[j]) * out[j]
                o_ref[q, at, :] = t
            panel = out[0]
            for i in range(1, PANEL):
                panel = jnp.where(sub == i, out[i], panel)
            o_ref[q, pl.ds(pl.multiple_of(base, SUB), SUB), :] = panel
        return c

    lax.fori_loop(0, n // PANEL, step, 0)


def bias_kernel(plan, dims, vis_ref, near_ref, far_ref, sol_ref, cov_ref, part_ref, tab_ref, hi_ref, lo_ref):
    stations, slots, n, width = dims
    half = near_ref.shape[0]
    for p in range(NHALF):
        x = near_ref[p] if p < half else far_ref[p - half]
        tab_ref[p] = x
        hi_ref[p], lo_ref[p] = split(x)
    mask = plan.mask()
    first = lax.axis_index("station") * plan.per
    for b in range(plan.per):
        cov_ref[b] = tab_ref[plan.position(first + b, mask)]

    def one(s):
        total = jnp.zeros((n, n), f32)
        for j in range(slots):
            v = vis_ref[s, j]
            at = plan.position(jnp.minimum(v, NHALF - 1), mask)
            x = split(sol_ref[s, j] * jnp.where(v < NHALF, 1.0, 0.0))
            lifted = dot3(x, (hi_ref[at], lo_ref[at]), NN)
            total = total + dot3(split(lifted), x, NT)
        return total

    pairs = stations // 2

    def pair(s, c):
        part_ref[pl.ds(pl.multiple_of(s * n, SUB), n), 0:n] = one(s)
        part_ref[pl.ds(pl.multiple_of(s * n, SUB), n), 64:64 + n] = one(s + pairs)
        return c

    lax.fori_loop(0, pairs, pair, 0)


def last_kernel(dims, len_ref, uni_ref, inv_ref, a_ref, b_ref, o_ref, map_ref, res_ref):
    stations, slots, n, width = dims
    for i in range(n):
        map_ref[pl.ds(i, stations, stride=n), :] = row_of(uni_ref, i, n).astype(f32)
    pairs = stations // 2
    r = lax.broadcasted_iota(jnp.int32, (n, n), 0)
    c = lax.broadcasted_iota(jnp.int32, (n, n), 1)
    for s in range(stations):
        keep = (r < len_ref[s]) & (c < len_ref[s])
        rows = slice((s % pairs) * n, (s % pairs) * n + n)
        cols = slice(0, n) if s < pairs else slice(64, 64 + n)
        part = a_ref[rows, cols] + b_ref[rows, cols]
        cov = jnp.where(keep, inv_ref[s * n:s * n + n, :n] + part, 0.0)
        z = map_ref[s * n:s * n + n, :n]
        zs = z.astype(bf16)
        hi, lo = split(cov)

        def d(x, y, dd):
            return lax.dot_general(x, y, (dd, ((), ())), preferred_element_type=f32)

        left = d(zs, hi, NN) + d(zs, lo, NN)
        hi, lo = split(left)
        res_ref[s * n:s * n + n, :n] = jnp.where(keep, d(hi, zs, NT) + d(lo, zs, NT), 0.0)
    for i in range(n):
        o_ref[:, i * n:i * n + n] = res_ref[pl.ds(i, stations, stride=n), :][:, :n]


def vmem():
    return pl.BlockSpec(memory_space=pltpu.VMEM)


def smem():
    return pl.BlockSpec(memory_space=pltpu.SMEM)


def local(plan, normal_mat, coupling, lengths, visible, bias_prior, unimod):
    stations, _, slots, n, width = coupling.shape
    dims = (stations, slots, n, width)
    cpl = coupling.reshape(dims)
    vis = visible.reshape(stations, slots)
    sds = jax.ShapeDtypeStruct
    sizes = []
    size = NHALF
    for _ in plan.steps:
        size //= 2
        sizes.append(size)
    sizes.append(size)
    inv, sol, *parts = pl.pallas_call(
        functools.partial(first_kernel, plan, dims),
        out_shape=[sds((stations * n, LANES), f32), sds(dims, f32)] + [sds((q, width, width), f32) for q in sizes],
        in_specs=[smem(), smem(), vmem(), vmem()],
        out_specs=[vmem()] * (2 + len(sizes)),
        scratch_shapes=[pltpu.VMEM((n, SUB, LANES), f32), pltpu.VMEM((NHALF + 1, width, width), f32)],
    )(lengths, vis, normal_mat, cpl)

    got = None
    for t, (axis, bit, _) in enumerate(plan.steps):
        send = parts[t]
        if got is not None:
            size = send.shape[0]
            send, got = send + got[size:], got[:size]
        new = lax.ppermute(send, axis, plan.perm(axis, bit))
        got = new if got is None else got + new
    keep = parts[-1]
    for axis, bit in plan.sums:
        total = got + keep
        got = lax.ppermute(total, axis, plan.perm(axis, bit))
        keep = total
    cov = pl.pallas_call(
        functools.partial(invert_kernel, plan),
        out_shape=sds(keep.shape, f32),
        in_specs=[vmem()] * 3,
        out_specs=vmem(),
    )(bias_prior.reshape(bias_prior.shape[1:]), keep, got)
    near, far = cov, None
    for axis, bit, _ in reversed(plan.steps):
        if far is not None:
            near = jnp.concatenate([near, far], 0)
        far = lax.ppermute(near, axis, plan.perm(axis, bit))
    bias_cov, part = pl.pallas_call(
        functools.partial(bias_kernel, plan, dims),
        out_shape=[sds((plan.per, width, width), f32), sds((stations // 2 * n, LANES), f32)],
        in_specs=[smem()] + [vmem()] * 3,
        out_specs=[vmem()] * 2,
        scratch_shapes=[pltpu.VMEM((NHALF, width, width), f32)] + [pltpu.VMEM((NHALF, width, width), bf16)] * 2,
    )(vis, near, far, sol)
    other = lax.ppermute(part, "bias", [(0, 1), (1, 0)])
    amb = pl.pallas_call(
        functools.partial(last_kernel, dims),
        out_shape=sds((stations, n * n), f32),
        in_specs=[smem()] + [vmem()] * 4,
        out_specs=vmem(),
        scratch_shapes=[pltpu.VMEM((stations * n, LANES), f32)] * 2,
    )(lengths, unimod, inv, part, other)
    return bias_cov.reshape((1,) + bias_cov.shape), amb


def solution(mesh):
    plan = Plan(mesh.shape["station"], mesh.shape["group"])
    return jax.shard_map(
        functools.partial(local, plan),
        mesh=mesh,
        in_specs=(
            P(("station", "group"), None),
            P(("station", "group"), "bias", None, None, None),
            P(("station", "group")),
            P(("station", "group"), "bias", None),
            P("bias", "station", None),
            P(("station", "group"), None),
        ),
        out_specs=(P("bias", "station", None, None), P(("station", "group"), None)),
        check_vma=False,
    )
```

```python
import functools

import jax
import jax.numpy as jnp
from jax import lax
from jax.experimental import pallas as pl
from jax.experimental.pallas import tpu as pltpu
from jax.sharding import PartitionSpec as P

NHALF = 16
LANES = 128
SUB = 8
PANEL = 8
f32 = jnp.float32
bf16 = jnp.bfloat16


def bits_of(n):
    count = n.bit_length() - 1
    assert 1 << count == n
    return count


class Plan:
    def __init__(self, stations, groups):
        per = max(NHALF // stations, 1)
        own = min(bits_of(per), bits_of(groups))
        steps = [("group", g, bits_of(per) - 1 - g) for g in range(own)]
        steps += [("station", z, bits_of(per) + z) for z in range(bits_of(stations))]
        self.per = per
        self.sizes = {"station": stations, "group": groups}
        self.steps = steps
        self.sums = [("group", g) for g in range(own, bits_of(groups))]
        used = [b for _, _, b in steps]
        rest = [b for b in range(bits_of(NHALF)) if b not in used]
        top = bits_of(NHALF) - 1
        self.moves = [(top - t, b) for t, b in enumerate(used)]
        self.moves += list(zip(range(len(rest)), sorted(rest)))
        self.left = NHALF >> len(steps)

    def mask(self):
        out = 0
        for axis, bit, block_bit in self.steps:
            out = out + (((lax.axis_index(axis) >> bit) & 1) << block_bit)
        return out

    def position(self, block, mask):
        y = block ^ mask
        out = 0
        for p, b in self.moves:
            out = out + (((y >> b) & 1) << p)
        return out

    def block(self, position, mask):
        out = 0
        for p, b in self.moves:
            out = out + (((position >> p) & 1) << b)
        return out ^ mask

    def perm(self, axis, bit):
        return [(i, i ^ (1 << bit)) for i in range(self.sizes[axis])]


def split(x):
    hi = x.astype(bf16)
    return hi, (x - hi.astype(f32)).astype(bf16)


def dot3(a, b, dims):
    def d(x, y):
        return lax.dot_general(x, y, (dims, ((), ())), preferred_element_type=f32)

    return d(a[0], b[0]) + (d(a[0], b[1]) + d(a[1], b[0]))


def split3(x):
    hi, rest = x.astype(bf16), None
    rest = x - hi.astype(f32)
    mid = rest.astype(bf16)
    return hi, mid, (rest - mid.astype(f32)).astype(bf16)


def dot6(a, b, dims):
    def d(x, y):
        return lax.dot_general(x, y, (dims, ((), ())), preferred_element_type=f32)

    small = d(a[0], b[2]) + (d(a[2], b[0]) + d(a[1], b[1]))
    return d(a[0], b[0]) + (d(a[0], b[1]) + (d(a[1], b[0]) + small))


NN = ((1,), (0,))
NT = ((1,), (1,))


def pick(x, idx):
    return jnp.take_along_axis(x, idx, axis=1)


def eliminate(rows, base, lane):
    b = len(rows)
    idx = [jnp.zeros((SUB, LANES), jnp.int32) + (base + j) for j in range(b)]
    p = [[pick(rows[i], idx[j]) for j in range(i + 1)] for i in range(b)]
    inside = (lane >= base) & (lane < base + b)
    y = [jnp.where(inside, (lane == base + i).astype(f32), rows[i]) for i in range(b)]
    l = [[None] * b for _ in range(b)]
    r = [None] * b
    for j in range(b):
        r[j] = 1.0 / p[j][j]
        for i in range(j + 1, b):
            l[i][j] = p[i][j] * r[j]
        for i in range(j + 1, b):
            for m in range(j + 1, i + 1):
                p[i][m] = p[i][m] - l[i][j] * p[m][j]
        for i in range(j + 1, b):
            y[i] = y[i] - l[i][j] * y[j]
    out = [None] * b
    for i in range(b - 1, -1, -1):
        t = y[i] * r[i]
        for j in range(b - 1, i, -1):
            t = t - l[j][i] * out[j]
        out[i] = t
    return out


def tile_iota(n):
    row = lax.broadcasted_iota(jnp.int32, (n, 2 * n), 0)
    lane = lax.broadcasted_iota(jnp.int32, (n, 2 * n), 1)
    return row, lane


def pack(x):
    n = x.shape[0] // 2
    row, lane = tile_iota(n)
    top, low = x[:n], x[n:]
    body = jnp.where((lane >= n) | (row >= lane), top, pltpu.roll(low, n, 1))
    diag = jnp.where(row == lane - n, low, 0.0)
    tail = diag[:SUB]
    for v in range(1, n // SUB):
        tail = tail + diag[v * SUB:v * SUB + SUB]
    return jnp.concatenate([body, tail], 0)


def unpack(y):
    n = y.shape[1] // 2
    row, lane = tile_iota(n)
    body, tail = y[:n], y[n:]
    top = jnp.where((lane >= n) | (row > lane), body, jnp.where(row == lane, 0.5 * body, 0.0))
    spread = jnp.concatenate([tail] * (n // SUB), 0)
    low = jnp.where(lane - n > row, pltpu.roll(body, n, 1), jnp.where(row == lane - n, 0.5 * spread, 0.0))
    return jnp.concatenate([top, low], 0)


def row_of(ref, i, n):
    at = i * n
    tile, off = at // LANES, at % LANES
    x = ref[:, tile * LANES:(tile + 1) * LANES]
    if off:
        x = pltpu.roll(x, LANES - off, 1)
        if off + n > LANES:
            nxt = ref[:, (tile + 1) * LANES:(tile + 2) * LANES]
            nxt = pltpu.roll(nxt, LANES - off, 1)
            lane = lax.broadcasted_iota(jnp.int32, (SUB, LANES), 1)
            x = jnp.where(lane < LANES - off, x, nxt)
    return x


def lengths_column(len_ref, stations):
    sub = lax.broadcasted_iota(jnp.int32, (SUB, LANES), 0)
    out = jnp.zeros((SUB, LANES), jnp.int32)
    for s in range(stations):
        out = jnp.where(sub == s, len_ref[s], out)
    return out


def first_kernel(plan, dims, len_ref, vis_ref, mat_ref, cpl_ref, inv_ref, sol_ref, *rest):
    stations, slots, n, width = dims
    outs, (pad_ref, acc_ref) = rest[:-2], rest[-2:]
    lane = lax.broadcasted_iota(jnp.int32, (SUB, LANES), 1)
    length = lengths_column(len_ref, stations)
    for i in range(n):
        x = row_of(mat_ref, i, n)
        keep = (lane < length) & (length > i)
        inv_ref[pl.ds(i, stations, stride=n), :] = jnp.where(keep, x, (lane == i).astype(f32))
    pad_ref[...] = jnp.zeros_like(pad_ref)
    wide = lax.broadcasted_iota(jnp.int32, (n, LANES), 1)

    def step(k, c):
        base = k * PANEL
        at = [pl.ds(base + i, stations, stride=n) for i in range(PANEL)]
        out = eliminate([inv_ref[at[i], :] for i in range(PANEL)], base, lane)
        for i in range(PANEL):
            pad_ref[at[i], :] = out[i]
        inside = (wide >= base) & (wide < base + PANEL)
        for s in range(stations):
            rows = slice(s * n, s * n + n)
            a = inv_ref[rows, :]
            r = pad_ref[rows, :]
            inv_ref[rows, :] = jnp.where(inside, 0.0, a) - dot6(split3(a[:, :n]), split3(r), NN)
        for i in range(PANEL):
            inv_ref[at[i], :] = out[i]
            pad_ref[at[i], :] = jnp.zeros((stations, LANES), f32)
        return c

    lax.fori_loop(0, n // PANEL, step, 0)
    acc_ref[...] = jnp.zeros_like(acc_ref)
    mask = plan.mask()
    tall = lax.broadcasted_iota(jnp.int32, (n, width), 0)

    def station(s, c):
        inverse = split(inv_ref[pl.ds(pl.multiple_of(s * n, SUB), n), :n])
        valid = tall < len_ref[s]
        for j in range(slots):
            w = jnp.where(valid, cpl_ref[s, j], 0.0)
            x = dot3(inverse, split(w), NN)
            sol_ref[s, j] = x
            red = dot3(split(w.T), split(w - x), NN)
            v = vis_ref[s, j]
            at = jnp.where(v < NHALF, plan.position(v, mask), NHALF)
            acc_ref[at] += red
        return c

    lax.fori_loop(0, stations, station, 0)
    at = NHALF
    for o in outs:
        at -= o.shape[0]
        for q in range(o.shape[0]):
            o[q] = pack(acc_ref[at + q])


def invert_kernel(plan, prior_ref, a_ref, b_ref, o_ref, x_ref):
    lane = lax.broadcasted_iota(jnp.int32, (SUB, LANES), 1)
    sub = lax.broadcasted_iota(jnp.int32, (SUB, LANES), 0)
    nb, n, _ = x_ref.shape
    mask = plan.mask()
    first = lax.axis_index("station") * plan.per
    row = lax.broadcasted_iota(jnp.int32, (n, n), 0)
    col = lax.broadcasted_iota(jnp.int32, (n, n), 1)
    for q in range(nb):
        prior = prior_ref[pl.ds(plan.block(q, mask) - first, 1), :]
        t = unpack(a_ref[q] + b_ref[q])
        x_ref[q] = t + t.T + jnp.where(row == col, jnp.broadcast_to(prior, (n, n)), 0.0)

    def step(k, c):
        base = k * PANEL
        for q in range(nb):
            rows = [jnp.broadcast_to(x_ref[q, pl.ds(base + i, 1), :], (SUB, LANES)) for i in range(PANEL)]
            out = eliminate(rows, base, lane)
            inside = (lane >= base) & (lane < base + PANEL)
            idx = [jnp.zeros((SUB, LANES), jnp.int32) + (base + j) for j in range(PANEL)]
            for v in range(n // SUB):
                at = slice(SUB * v, SUB * v + SUB)
                a = x_ref[q, at, :]
                t = jnp.where(inside, 0.0, a)
                for j in range(PANEL - 1, -1, -1):
                    t = t - pick(a, idx[j]) * out[j]
                x_ref[q, at, :] = t
            panel = out[0]
            for i in range(1, PANEL):
                panel = jnp.where(sub == i, out[i], panel)
            x_ref[q, pl.ds(pl.multiple_of(base, SUB), SUB), :] = panel
        return c

    lax.fori_loop(0, n // PANEL, step, 0)
    for q in range(nb):
        o_ref[q] = pack(x_ref[q])


def bias_kernel(plan, dims, vis_ref, near_ref, far_ref, sol_ref, cov_ref, part_ref, tab_ref, hi_ref, lo_ref):
    stations, slots, n, width = dims
    half = near_ref.shape[0]
    for p in range(NHALF):
        x = unpack(near_ref[p] if p < half else far_ref[p - half])
        tab_ref[p] = x
        hi_ref[p], lo_ref[p] = split(x)
    mask = plan.mask()
    first = lax.axis_index("station") * plan.per
    for b in range(plan.per):
        x = tab_ref[plan.position(first + b, mask)]
        cov_ref[b] = x + x.T

    def one(s):
        total = jnp.zeros((n, n), f32)
        for j in range(slots):
            v = vis_ref[s, j]
            at = plan.position(jnp.minimum(v, NHALF - 1), mask)
            x = split(sol_ref[s, j] * jnp.where(v < NHALF, 1.0, 0.0))
            lifted = dot3(x, (hi_ref[at], lo_ref[at]), NN)
            total = total + dot3(split(lifted), x, NT)
        return total + total.T

    pairs = stations // 2

    def pair(s, c):
        part_ref[pl.ds(pl.multiple_of(s * n, SUB), n), 0:n] = one(s)
        part_ref[pl.ds(pl.multiple_of(s * n, SUB), n), 64:64 + n] = one(s + pairs)
        return c

    lax.fori_loop(0, pairs, pair, 0)


def last_kernel(dims, len_ref, uni_ref, inv_ref, a_ref, b_ref, o_ref, map_ref, res_ref):
    stations, slots, n, width = dims
    for i in range(n):
        map_ref[pl.ds(i, stations, stride=n), :] = row_of(uni_ref, i, n).astype(f32)
    pairs = stations // 2
    r = lax.broadcasted_iota(jnp.int32, (n, n), 0)
    c = lax.broadcasted_iota(jnp.int32, (n, n), 1)
    for s in range(stations):
        keep = (r < len_ref[s]) & (c < len_ref[s])
        rows = slice((s % pairs) * n, (s % pairs) * n + n)
        cols = slice(0, n) if s < pairs else slice(64, 64 + n)
        part = a_ref[rows, cols] + b_ref[rows, cols]
        cov = jnp.where(keep, inv_ref[s * n:s * n + n, :n] + part, 0.0)
        z = map_ref[s * n:s * n + n, :n]
        zs = z.astype(bf16)
        hi, lo = split(cov)

        def d(x, y, dd):
            return lax.dot_general(x, y, (dd, ((), ())), preferred_element_type=f32)

        left = d(zs, hi, NN) + d(zs, lo, NN)
        hi, lo = split(left)
        res_ref[s * n:s * n + n, :n] = jnp.where(keep, d(hi, zs, NT) + d(lo, zs, NT), 0.0)
    for i in range(n):
        o_ref[:, i * n:i * n + n] = res_ref[pl.ds(i, stations, stride=n), :][:, :n]


def vmem():
    return pl.BlockSpec(memory_space=pltpu.VMEM)


def smem():
    return pl.BlockSpec(memory_space=pltpu.SMEM)


def local(plan, normal_mat, coupling, lengths, visible, bias_prior, unimod):
    stations, _, slots, n, width = coupling.shape
    dims = (stations, slots, n, width)
    cpl = coupling.reshape(dims)
    vis = visible.reshape(stations, slots)
    sds = jax.ShapeDtypeStruct
    sizes = []
    size = NHALF
    for _ in plan.steps:
        size //= 2
        sizes.append(size)
    sizes.append(size)
    inv, sol, *parts = pl.pallas_call(
        functools.partial(first_kernel, plan, dims),
        out_shape=[sds((stations * n, LANES), f32), sds(dims, f32)] + [sds((q, width // 2 + SUB, width), f32) for q in sizes],
        in_specs=[smem(), smem(), vmem(), vmem()],
        out_specs=[vmem()] * (2 + len(sizes)),
        scratch_shapes=[pltpu.VMEM((stations * n, LANES), f32), pltpu.VMEM((NHALF + 1, width, width), f32)],
    )(lengths, vis, normal_mat, cpl)

    got = None
    for t, (axis, bit, _) in enumerate(plan.steps):
        send = parts[t]
        if got is not None:
            size = send.shape[0]
            send, got = send + got[size:], got[:size]
        new = lax.ppermute(send, axis, plan.perm(axis, bit))
        got = new if got is None else got + new
    keep = parts[-1]
    for axis, bit in plan.sums:
        total = got + keep
        got = lax.ppermute(total, axis, plan.perm(axis, bit))
        keep = total
    cov = pl.pallas_call(
        functools.partial(invert_kernel, plan),
        out_shape=sds(keep.shape, f32),
        in_specs=[vmem()] * 3,
        out_specs=vmem(),
        scratch_shapes=[pltpu.VMEM((keep.shape[0], width, width), f32)],
    )(bias_prior.reshape(bias_prior.shape[1:]), keep, got)
    near, far = cov, None
    for axis, bit, _ in reversed(plan.steps):
        if far is not None:
            near = jnp.concatenate([near, far], 0)
        far = lax.ppermute(near, axis, plan.perm(axis, bit))
    bias_cov, part = pl.pallas_call(
        functools.partial(bias_kernel, plan, dims),
        out_shape=[sds((plan.per, width, width), f32), sds((stations // 2 * n, LANES), f32)],
        in_specs=[smem()] + [vmem()] * 3,
        out_specs=[vmem()] * 2,
        scratch_shapes=[pltpu.VMEM((NHALF, width, width), f32)] + [pltpu.VMEM((NHALF, width, width), bf16)] * 2,
    )(vis, near, far, sol)
    other = lax.ppermute(part, "bias", [(0, 1), (1, 0)])
    amb = pl.pallas_call(
        functools.partial(last_kernel, dims),
        out_shape=sds((stations, n * n), f32),
        in_specs=[smem()] + [vmem()] * 4,
        out_specs=vmem(),
        scratch_shapes=[pltpu.VMEM((stations * n, LANES), f32)] * 2,
    )(lengths, unimod, inv, part, other)
    return bias_cov.reshape((1,) + bias_cov.shape), amb


def solution(mesh):
    plan = Plan(mesh.shape["station"], mesh.shape["group"])
    return jax.shard_map(
        functools.partial(local, plan),
        mesh=mesh,
        in_specs=(
            P(("station", "group"), None),
            P(("station", "group"), "bias", None, None, None),
            P(("station", "group")),
            P(("station", "group"), "bias", None),
            P("bias", "station", None),
            P(("station", "group"), None),
        ),
        out_specs=(P("bias", "station", None, None), P(("station", "group"), None)),
        check_vma=False,
    )
```

```python
import functools

import jax
import jax.numpy as jnp
from jax import lax
from jax.experimental import pallas as pl
from jax.experimental.pallas import tpu as pltpu
from jax.sharding import PartitionSpec as P

NHALF = 16
LANES = 128
SUB = 8
PANEL = 8
f32 = jnp.float32
bf16 = jnp.bfloat16

PARAMS = pltpu.CompilerParams(vmem_limit_bytes=16 << 20)


def bits_of(n):
    count = n.bit_length() - 1
    assert 1 << count == n
    return count


class Plan:
    def __init__(self, stations, groups):
        per = max(NHALF // stations, 1)
        own = min(bits_of(per), bits_of(groups))
        steps = [("group", g, bits_of(per) - 1 - g) for g in range(own)]
        steps += [("station", z, bits_of(per) + z) for z in range(bits_of(stations))]
        self.per = per
        self.sizes = {"station": stations, "group": groups}
        self.steps = steps
        self.sums = [("group", g) for g in range(own, bits_of(groups))]
        used = [b for _, _, b in steps]
        rest = [b for b in range(bits_of(NHALF)) if b not in used]
        top = bits_of(NHALF) - 1
        self.moves = [(top - t, b) for t, b in enumerate(used)]
        self.moves += list(zip(range(len(rest)), sorted(rest)))
        self.left = NHALF >> len(steps)

    def mask(self):
        out = 0
        for axis, bit, block_bit in self.steps:
            out = out + (((lax.axis_index(axis) >> bit) & 1) << block_bit)
        return out

    def position(self, block, mask):
        y = block ^ mask
        out = 0
        for p, b in self.moves:
            out = out + (((y >> b) & 1) << p)
        return out

    def block(self, position, mask):
        out = 0
        for p, b in self.moves:
            out = out + (((position >> p) & 1) << b)
        return out ^ mask

    def perm(self, axis, bit):
        return [(i, i ^ (1 << bit)) for i in range(self.sizes[axis])]


def split(x):
    hi = x.astype(bf16)
    return hi, (x - hi.astype(f32)).astype(bf16)


def dot3(a, b, dims):
    def d(x, y):
        return lax.dot_general(x, y, (dims, ((), ())), preferred_element_type=f32)

    return d(a[0], b[0]) + (d(a[0], b[1]) + d(a[1], b[0]))


def split3(x):
    hi, rest = x.astype(bf16), None
    rest = x - hi.astype(f32)
    mid = rest.astype(bf16)
    return hi, mid, (rest - mid.astype(f32)).astype(bf16)


def dot6(a, b, dims):
    def d(x, y):
        return lax.dot_general(x, y, (dims, ((), ())), preferred_element_type=f32)

    small = d(a[0], b[2]) + (d(a[2], b[0]) + d(a[1], b[1]))
    return d(a[0], b[0]) + (d(a[0], b[1]) + (d(a[1], b[0]) + small))


NN = ((1,), (0,))
NT = ((1,), (1,))


def mxu(a, b, dims):
    return lax.dot_general(a, b, (dims, ((), ())), preferred_element_type=f32)


def stacked(x, axis):
    return jnp.concatenate(split(x), axis)


def corner(y, m, n):
    return y[:m, :n] + (y[:m, n:] + y[m:, :n])


def pick(x, idx):
    return jnp.take_along_axis(x, idx, axis=1)


def eliminate(rows, base, lane):
    b = len(rows)
    idx = [jnp.zeros((SUB, LANES), jnp.int32) + (base + j) for j in range(b)]
    p = [[pick(rows[i], idx[j]) for j in range(i + 1)] for i in range(b)]
    inside = (lane >= base) & (lane < base + b)
    y = [jnp.where(inside, (lane == base + i).astype(f32), rows[i]) for i in range(b)]
    l = [[None] * b for _ in range(b)]
    r = [None] * b
    for j in range(b):
        r[j] = 1.0 / p[j][j]
        for i in range(j + 1, b):
            l[i][j] = p[i][j] * r[j]
        for i in range(j + 1, b):
            for m in range(j + 1, i + 1):
                p[i][m] = p[i][m] - l[i][j] * p[m][j]
        for i in range(j + 1, b):
            y[i] = y[i] - l[i][j] * y[j]
    out = [None] * b
    for i in range(b - 1, -1, -1):
        t = y[i] * r[i]
        for j in range(b - 1, i, -1):
            t = t - l[j][i] * out[j]
        out[i] = t
    return out


def tile_iota(n):
    row = lax.broadcasted_iota(jnp.int32, (n, 2 * n), 0)
    lane = lax.broadcasted_iota(jnp.int32, (n, 2 * n), 1)
    return row, lane


def pack(x):
    n = x.shape[0] // 2
    row, lane = tile_iota(n)
    top, low = x[:n], x[n:]
    body = jnp.where((lane >= n) | (row >= lane), top, pltpu.roll(low, n, 1))
    diag = jnp.where(row == lane - n, low, 0.0)
    tail = diag[:SUB]
    for v in range(1, n // SUB):
        tail = tail + diag[v * SUB:v * SUB + SUB]
    return jnp.concatenate([body, tail], 0)


def unpack(y):
    n = y.shape[1] // 2
    row, lane = tile_iota(n)
    body, tail = y[:n], y[n:]
    top = jnp.where((lane >= n) | (row > lane), body, jnp.where(row == lane, 0.5 * body, 0.0))
    spread = jnp.concatenate([tail] * (n // SUB), 0)
    low = jnp.where(lane - n > row, pltpu.roll(body, n, 1), jnp.where(row == lane - n, 0.5 * spread, 0.0))
    return jnp.concatenate([top, low], 0)


def row_of(ref, i, n):
    at = i * n
    tile, off = at // LANES, at % LANES
    x = ref[:, tile * LANES:(tile + 1) * LANES]
    if off:
        x = pltpu.roll(x, LANES - off, 1)
        if off + n > LANES:
            nxt = ref[:, (tile + 1) * LANES:(tile + 2) * LANES]
            nxt = pltpu.roll(nxt, LANES - off, 1)
            lane = lax.broadcasted_iota(jnp.int32, (SUB, LANES), 1)
            x = jnp.where(lane < LANES - off, x, nxt)
    return x


def lengths_column(len_ref, stations):
    sub = lax.broadcasted_iota(jnp.int32, (SUB, LANES), 0)
    out = jnp.zeros((SUB, LANES), jnp.int32)
    for s in range(stations):
        out = jnp.where(sub == s, len_ref[s], out)
    return out


def first_kernel(plan, dims, len_ref, vis_ref, mat_ref, cpl_ref, inv_ref, sol_ref, *rest):
    stations, slots, n, width = dims
    outs, (pad_ref, acc_ref) = rest[:-2], rest[-2:]
    lane = lax.broadcasted_iota(jnp.int32, (SUB, LANES), 1)
    length = lengths_column(len_ref, stations)
    for i in range(n):
        x = row_of(mat_ref, i, n)
        keep = (lane < length) & (length > i)
        inv_ref[pl.ds(i, stations, stride=n), :] = jnp.where(keep, x, (lane == i).astype(f32))
    pad_ref[...] = jnp.zeros_like(pad_ref)
    wide = lax.broadcasted_iota(jnp.int32, (n, LANES), 1)

    def step(k, c):
        base = k * PANEL
        at = [pl.ds(base + i, stations, stride=n) for i in range(PANEL)]
        out = eliminate([inv_ref[at[i], :] for i in range(PANEL)], base, lane)
        for i in range(PANEL):
            pad_ref[at[i], :] = out[i]
        inside = (wide >= base) & (wide < base + PANEL)
        for s in range(stations):
            rows = slice(s * n, s * n + n)
            a = inv_ref[rows, :]
            r = pad_ref[rows, :]
            inv_ref[rows, :] = jnp.where(inside, 0.0, a) - dot6(split3(a[:, :n]), split3(r), NN)
        for i in range(PANEL):
            inv_ref[at[i], :] = out[i]
            pad_ref[at[i], :] = jnp.zeros((stations, LANES), f32)
        return c

    lax.fori_loop(0, n // PANEL, step, 0)
    acc_ref[...] = jnp.zeros_like(acc_ref)
    mask = plan.mask()
    tall = lax.broadcasted_iota(jnp.int32, (n, width), 0)

    def station(s, c):
        inverse = stacked(inv_ref[pl.ds(pl.multiple_of(s * n, SUB), n), :n], 0)
        valid = tall < len_ref[s]
        for j in range(slots):
            w = jnp.where(valid, cpl_ref[s, j], 0.0)
            hi, lo = split(w)
            x = corner(mxu(inverse, jnp.concatenate([hi, lo], 1), NN), n, width)
            sol_ref[s, j] = x
            tall_w = jnp.concatenate([hi.astype(f32), lo.astype(f32)], 0).T.astype(bf16)
            d = stacked(w - x, 1)
            red = mxu(tall_w, jnp.concatenate([d, d], 0), NN)
            v = vis_ref[s, j]
            at = jnp.where(v < NHALF, plan.position(v, mask), NHALF)
            acc_ref[at] += red[:, :width] + red[:, width:]
        return c

    lax.fori_loop(0, stations, station, 0)
    at = NHALF
    for o in outs:
        at -= o.shape[0]
        for q in range(o.shape[0]):
            o[q] = pack(acc_ref[at + q])


def invert_kernel(plan, prior_ref, a_ref, b_ref, o_ref, x_ref, pad_ref, cur_ref):
    lane = lax.broadcasted_iota(jnp.int32, (SUB, LANES), 1)
    sub = lax.broadcasted_iota(jnp.int32, (SUB, LANES), 0)
    nb, n, _ = x_ref.shape
    mask = plan.mask()
    first = lax.axis_index("station") * plan.per
    row = lax.broadcasted_iota(jnp.int32, (n, n), 0)
    col = lax.broadcasted_iota(jnp.int32, (n, n), 1)
    for q in range(nb):
        prior = prior_ref[pl.ds(plan.block(q, mask) - first, 1), :]
        t = unpack(a_ref[q] + b_ref[q])
        x = t + t.T + jnp.where(row == col, jnp.broadcast_to(prior, (n, n)), 0.0)
        x_ref[q] = x
        cur_ref[q] = x[:PANEL]
    pad_ref[...] = jnp.zeros_like(pad_ref)

    def update(q, prev):
        a, r = x_ref[q], pad_ref[q]
        inside = (col >= prev) & (col < prev + PANEL)
        a = jnp.where(inside, 0.0, a) - dot6(split3(a), split3(r), NN)
        return jnp.where((row >= prev) & (row < prev + PANEL), r, a)

    def step(k, c):
        base = k * PANEL
        inside = (lane >= base) & (lane < base + PANEL)
        for q in range(nb):
            rows = [jnp.broadcast_to(cur_ref[q, i:i + 1, :], (SUB, LANES)) for i in range(PANEL)]
            out = eliminate(rows, base, lane)
            x_ref[q] = update(q, base - PANEL)
            y = x_ref[q, pl.ds(pl.multiple_of(jnp.minimum(base + PANEL, n - PANEL), PANEL), PANEL), :]
            t = jnp.where(inside, 0.0, y)
            for j in range(PANEL - 1, -1, -1):
                t = t - pick(y, jnp.zeros((SUB, LANES), jnp.int32) + (base + j)) * out[j]
            cur_ref[q] = t
            pad_ref[q, pl.ds(pl.multiple_of(jnp.maximum(base - PANEL, 0), PANEL), PANEL), :] = jnp.zeros((SUB, LANES), f32)
            panel = out[0]
            for i in range(1, PANEL):
                panel = jnp.where(sub == i, out[i], panel)
            pad_ref[q, pl.ds(pl.multiple_of(base, PANEL), PANEL), :] = panel
        return c

    lax.fori_loop(0, n // PANEL, step, 0)
    for q in range(nb):
        o_ref[q] = pack(update(q, n - PANEL))


def bias_kernel(plan, dims, vis_ref, near_ref, far_ref, sol_ref, cov_ref, part_ref, tab_ref, two_ref):
    stations, slots, n, width = dims
    half = near_ref.shape[0]
    for p in range(NHALF):
        x = unpack(near_ref[p] if p < half else far_ref[p - half])
        tab_ref[p] = x
        two_ref[p] = stacked(x, 1)
    mask = plan.mask()
    first = lax.axis_index("station") * plan.per
    for b in range(plan.per):
        x = tab_ref[plan.position(first + b, mask)]
        cov_ref[b] = x + x.T

    def one(s):
        hi, lo, lifted = [], [], []
        for j in range(slots):
            v = vis_ref[s, j]
            at = plan.position(jnp.minimum(v, NHALF - 1), mask)
            x = split(sol_ref[s, j] * jnp.where(v < NHALF, 1.0, 0.0))
            hi.append(x[0])
            lo.append(x[1])
            lifted.append(corner(mxu(jnp.concatenate(x, 0), two_ref[at], NN), n, width))
        right = jnp.concatenate([jnp.concatenate(hi, 1), jnp.concatenate(lo, 1)], 0)
        total = corner(mxu(stacked(jnp.concatenate(lifted, 1), 0), right, NT), n, n)
        return total + total.T

    pairs = stations // 2

    def pair(s, c):
        part_ref[pl.ds(pl.multiple_of(s * n, SUB), n), 0:n] = one(s)
        part_ref[pl.ds(pl.multiple_of(s * n, SUB), n), 64:64 + n] = one(s + pairs)
        return c

    lax.fori_loop(0, pairs, pair, 0)


def last_kernel(dims, len_ref, uni_ref, inv_ref, a_ref, b_ref, o_ref, map_ref, res_ref):
    stations, slots, n, width = dims
    for i in range(n):
        map_ref[pl.ds(i, stations, stride=n), :] = row_of(uni_ref, i, n).astype(f32)
    pairs = stations // 2
    r = lax.broadcasted_iota(jnp.int32, (n, n), 0)
    c = lax.broadcasted_iota(jnp.int32, (n, n), 1)
    for s in range(stations):
        keep = (r < len_ref[s]) & (c < len_ref[s])
        rows = slice((s % pairs) * n, (s % pairs) * n + n)
        cols = slice(0, n) if s < pairs else slice(64, 64 + n)
        part = a_ref[rows, cols] + b_ref[rows, cols]
        cov = jnp.where(keep, inv_ref[s * n:s * n + n, :n] + part, 0.0)
        z = map_ref[s * n:s * n + n, :n]
        zs = z.astype(bf16)
        hi, lo = split(cov)

        def d(x, y, dd):
            return lax.dot_general(x, y, (dd, ((), ())), preferred_element_type=f32)

        left = d(zs, hi, NN) + d(zs, lo, NN)
        hi, lo = split(left)
        res_ref[s * n:s * n + n, :n] = jnp.where(keep, d(hi, zs, NT) + d(lo, zs, NT), 0.0)
    for i in range(n):
        o_ref[:, i * n:i * n + n] = res_ref[pl.ds(i, stations, stride=n), :][:, :n]


def vmem():
    return pl.BlockSpec(memory_space=pltpu.VMEM)


def smem():
    return pl.BlockSpec(memory_space=pltpu.SMEM)


def local(plan, normal_mat, coupling, lengths, visible, bias_prior, unimod):
    stations, _, slots, n, width = coupling.shape
    dims = (stations, slots, n, width)
    cpl = coupling.reshape(dims)
    vis = visible.reshape(stations, slots)
    sds = jax.ShapeDtypeStruct
    sizes = []
    size = NHALF
    for _ in plan.steps:
        size //= 2
        sizes.append(size)
    sizes.append(size)
    inv, sol, *parts = pl.pallas_call(
        functools.partial(first_kernel, plan, dims),
        out_shape=[sds((stations * n, LANES), f32), sds(dims, f32)] + [sds((q, width // 2 + SUB, width), f32) for q in sizes],
        in_specs=[smem(), smem(), vmem(), vmem()],
        out_specs=[vmem()] * (2 + len(sizes)),
        scratch_shapes=[pltpu.VMEM((stations * n, LANES), f32), pltpu.VMEM((NHALF + 1, width, width), f32)],
        compiler_params=PARAMS,
    )(lengths, vis, normal_mat, cpl)

    got = None
    for t, (axis, bit, _) in enumerate(plan.steps):
        send = parts[t]
        if got is not None:
            size = send.shape[0]
            send, got = send + got[size:], got[:size]
        new = lax.ppermute(send, axis, plan.perm(axis, bit))
        got = new if got is None else got + new
    keep = parts[-1]
    for axis, bit in plan.sums:
        total = got + keep
        got = lax.ppermute(total, axis, plan.perm(axis, bit))
        keep = total
    cov = pl.pallas_call(
        functools.partial(invert_kernel, plan),
        out_shape=sds(keep.shape, f32),
        in_specs=[vmem()] * 3,
        out_specs=vmem(),
        scratch_shapes=[pltpu.VMEM((keep.shape[0], width, width), f32)] * 2 + [pltpu.VMEM((keep.shape[0], PANEL, width), f32)],
        compiler_params=PARAMS,
    )(bias_prior.reshape(bias_prior.shape[1:]), keep, got)
    near, far = cov, None
    for axis, bit, _ in reversed(plan.steps):
        if far is not None:
            near = jnp.concatenate([near, far], 0)
        far = lax.ppermute(near, axis, plan.perm(axis, bit))
    bias_cov, part = pl.pallas_call(
        functools.partial(bias_kernel, plan, dims),
        out_shape=[sds((plan.per, width, width), f32), sds((stations // 2 * n, LANES), f32)],
        in_specs=[smem()] + [vmem()] * 3,
        out_specs=[vmem()] * 2,
        scratch_shapes=[pltpu.VMEM((NHALF, width, width), f32), pltpu.VMEM((NHALF, width, 2 * width), bf16)],
        compiler_params=PARAMS,
    )(vis, near, far, sol)
    other = lax.ppermute(part, "bias", [(0, 1), (1, 0)])
    amb = pl.pallas_call(
        functools.partial(last_kernel, dims),
        out_shape=sds((stations, n * n), f32),
        in_specs=[smem()] + [vmem()] * 4,
        out_specs=vmem(),
        scratch_shapes=[pltpu.VMEM((stations * n, LANES), f32)] * 2,
        compiler_params=PARAMS,
    )(lengths, unimod, inv, part, other)
    return bias_cov.reshape((1,) + bias_cov.shape), amb


def solution(mesh):
    plan = Plan(mesh.shape["station"], mesh.shape["group"])
    return jax.shard_map(
        functools.partial(local, plan),
        mesh=mesh,
        in_specs=(
            P(("station", "group"), None),
            P(("station", "group"), "bias", None, None, None),
            P(("station", "group")),
            P(("station", "group"), "bias", None),
            P("bias", "station", None),
            P(("station", "group"), None),
        ),
        out_specs=(P("bias", "station", None, None), P(("station", "group"), None)),
        check_vma=False,
    )
```

```python
import functools

import jax
import jax.numpy as jnp
from jax import lax
from jax.experimental import pallas as pl
from jax.experimental.pallas import tpu as pltpu
from jax.sharding import PartitionSpec as P

NHALF = 16
LANES = 128
SUB = 8
PANEL = 8
f32 = jnp.float32
bf16 = jnp.bfloat16

PARAMS = pltpu.CompilerParams(vmem_limit_bytes=16 << 20)


def bits_of(n):
    count = n.bit_length() - 1
    assert 1 << count == n
    return count


class Plan:
    def __init__(self, stations, groups):
        per = max(NHALF // stations, 1)
        own = min(bits_of(per), bits_of(groups))
        steps = [("group", g, bits_of(per) - 1 - g) for g in range(own)]
        steps += [("station", z, bits_of(per) + z) for z in range(bits_of(stations))]
        self.per = per
        self.sizes = {"station": stations, "group": groups}
        self.steps = steps
        self.sums = [("group", g) for g in range(own, bits_of(groups))]
        used = [b for _, _, b in steps]
        rest = [b for b in range(bits_of(NHALF)) if b not in used]
        top = bits_of(NHALF) - 1
        self.moves = [(top - t, b) for t, b in enumerate(used)]
        self.moves += list(zip(range(len(rest)), sorted(rest)))
        self.left = NHALF >> len(steps)

    def mask(self):
        out = 0
        for axis, bit, block_bit in self.steps:
            out = out + (((lax.axis_index(axis) >> bit) & 1) << block_bit)
        return out

    def position(self, block, mask):
        y = block ^ mask
        out = 0
        for p, b in self.moves:
            out = out + (((y >> b) & 1) << p)
        return out

    def block(self, position, mask):
        out = 0
        for p, b in self.moves:
            out = out + (((position >> p) & 1) << b)
        return out ^ mask

    def perm(self, axis, bit):
        return [(i, i ^ (1 << bit)) for i in range(self.sizes[axis])]


def split(x):
    hi = x.astype(bf16)
    return hi, (x - hi.astype(f32)).astype(bf16)


def dot3(a, b, dims):
    def d(x, y):
        return lax.dot_general(x, y, (dims, ((), ())), preferred_element_type=f32)

    return d(a[0], b[0]) + (d(a[0], b[1]) + d(a[1], b[0]))


def split3(x):
    hi = x.astype(bf16).astype(f32)
    rest = x - hi
    mid = rest.astype(bf16).astype(f32)
    return hi, mid, rest - mid


def left_of(x):
    hi, mid, lo = split3(x)
    return jnp.concatenate([hi, hi, mid, hi, lo, mid], 0).T.astype(bf16)


def right_of(r):
    hi, mid, lo = split3(r)
    return jnp.concatenate([hi, mid, hi, lo, hi, mid], 0).astype(bf16)


NN = ((1,), (0,))
NT = ((1,), (1,))


def mxu(a, b, dims):
    return lax.dot_general(a, b, (dims, ((), ())), preferred_element_type=f32)


def stacked(x, axis):
    return jnp.concatenate(split(x), axis)


def corner(y, m, n):
    return y[:m, :n] + (y[:m, n:] + y[m:, :n])


def pick(x, idx):
    return jnp.take_along_axis(x, idx, axis=1)


def eliminate(rows, base, lane):
    b = len(rows)
    idx = [jnp.zeros((SUB, LANES), jnp.int32) + (base + j) for j in range(b)]
    p = [[pick(rows[i], idx[j]) for j in range(i + 1)] for i in range(b)]
    inside = (lane >= base) & (lane < base + b)
    y = [jnp.where(inside, (lane == base + i).astype(f32), rows[i]) for i in range(b)]
    l = [[None] * b for _ in range(b)]
    r = [None] * b
    for j in range(b):
        r[j] = 1.0 / p[j][j]
        for i in range(j + 1, b):
            l[i][j] = p[i][j] * r[j]
        for i in range(j + 1, b):
            for m in range(j + 1, i + 1):
                p[i][m] = p[i][m] - l[i][j] * p[m][j]
        for i in range(j + 1, b):
            y[i] = y[i] - l[i][j] * y[j]
    out = [None] * b
    for i in range(b - 1, -1, -1):
        t = y[i] * r[i]
        for j in range(b - 1, i, -1):
            t = t - l[j][i] * out[j]
        out[i] = t
    return out


def tile_iota(n):
    row = lax.broadcasted_iota(jnp.int32, (n, 2 * n), 0)
    lane = lax.broadcasted_iota(jnp.int32, (n, 2 * n), 1)
    return row, lane


def pack(x):
    n = x.shape[0] // 2
    row, lane = tile_iota(n)
    top, low = x[:n], x[n:]
    body = jnp.where((lane >= n) | (row >= lane), top, pltpu.roll(low, n, 1))
    diag = jnp.where(row == lane - n, low, 0.0)
    tail = diag[:SUB]
    for v in range(1, n // SUB):
        tail = tail + diag[v * SUB:v * SUB + SUB]
    return jnp.concatenate([body, tail], 0)


def unpack(y):
    n = y.shape[1] // 2
    row, lane = tile_iota(n)
    body, tail = y[:n], y[n:]
    top = jnp.where((lane >= n) | (row > lane), body, jnp.where(row == lane, 0.5 * body, 0.0))
    spread = jnp.concatenate([tail] * (n // SUB), 0)
    low = jnp.where(lane - n > row, pltpu.roll(body, n, 1), jnp.where(row == lane - n, 0.5 * spread, 0.0))
    return jnp.concatenate([top, low], 0)


def row_of(ref, i, n):
    at = i * n
    tile, off = at // LANES, at % LANES
    x = ref[:, tile * LANES:(tile + 1) * LANES]
    if off:
        x = pltpu.roll(x, LANES - off, 1)
        if off + n > LANES:
            nxt = ref[:, (tile + 1) * LANES:(tile + 2) * LANES]
            nxt = pltpu.roll(nxt, LANES - off, 1)
            lane = lax.broadcasted_iota(jnp.int32, (SUB, LANES), 1)
            x = jnp.where(lane < LANES - off, x, nxt)
    return x


def lengths_column(len_ref, stations):
    sub = lax.broadcasted_iota(jnp.int32, (SUB, LANES), 0)
    out = jnp.zeros((SUB, LANES), jnp.int32)
    for s in range(stations):
        out = jnp.where(sub == s, len_ref[s], out)
    return out


def first_kernel(plan, dims, len_hbm, vis_hbm, mat_hbm, cpl_hbm, inv_ref, sol_ref, *rest):
    stations, slots, n, width = dims
    outs, (len_ref, vis_ref, mat_ref, cpl_ref, pad_ref, acc_ref, sem) = rest[:-7], rest[-7:]
    pairs = ((len_hbm, len_ref), (mat_hbm, mat_ref), (vis_hbm, vis_ref), (cpl_hbm, cpl_ref))
    loads = [pltpu.make_async_copy(src, dst, sem.at[t]) for t, (src, dst) in enumerate(pairs)]
    for load in loads:
        load.start()
    acc_ref[...] = jnp.zeros_like(acc_ref)
    loads[0].wait()
    loads[1].wait()
    lane = lax.broadcasted_iota(jnp.int32, (SUB, LANES), 1)
    length = lengths_column(len_ref, stations)
    for i in range(n):
        x = row_of(mat_ref, i, n)
        keep = (lane < length) & (length > i)
        inv_ref[pl.ds(i, stations, stride=n), :] = jnp.where(keep, x, (lane == i).astype(f32))
    wide = lax.broadcasted_iota(jnp.int32, (n, LANES), 1)

    def step(k, c):
        base = k * PANEL
        at = [pl.ds(base + i, stations, stride=n) for i in range(PANEL)]
        out = eliminate([inv_ref[at[i], :] for i in range(PANEL)], base, lane)
        for i in range(PANEL):
            pad_ref[pl.ds(i, stations, stride=PANEL), :] = out[i]
        inside = (wide >= base) & (wide < base + PANEL)
        for s in range(stations):
            rows = slice(s * n, s * n + n)
            x = inv_ref[pl.ds(pl.multiple_of(s * n + base, PANEL), PANEL), :]
            left = left_of(jnp.where(lane < base, -x, x)[:, :n])
            right = right_of(pad_ref[s * PANEL:s * PANEL + PANEL, :])
            inv_ref[rows, :] = jnp.where(inside, 0.0, inv_ref[rows, :]) - mxu(left, right, NN)
        for i in range(PANEL):
            inv_ref[at[i], :] = out[i]
        return c

    lax.fori_loop(0, n // PANEL, step, 0)
    loads[2].wait()
    loads[3].wait()
    mask = plan.mask()
    tall = lax.broadcasted_iota(jnp.int32, (n, width), 0)

    def station(s, c):
        inverse = stacked(inv_ref[pl.ds(pl.multiple_of(s * n, SUB), n), :n], 0)
        valid = tall < len_ref[s]
        for j in range(slots):
            w = jnp.where(valid, cpl_ref[s, j], 0.0)
            hi, lo = split(w)
            x = corner(mxu(inverse, jnp.concatenate([hi, lo], 1), NN), n, width)
            sol_ref[s, j] = x
            tall_w = jnp.concatenate([hi.astype(f32), lo.astype(f32)], 0).T.astype(bf16)
            d = stacked(w - x, 1)
            red = mxu(tall_w, jnp.concatenate([d, d], 0), NN)
            v = vis_ref[s, j]
            at = jnp.where(v < NHALF, plan.position(v, mask), NHALF)
            acc_ref[at] += red[:, :width] + red[:, width:]
        return c

    lax.fori_loop(0, stations, station, 0)
    at = NHALF
    for o in outs:
        at -= o.shape[0]
        for q in range(o.shape[0]):
            o[q] = pack(acc_ref[at + q])


def invert_kernel(plan, prior_ref, a_ref, b_ref, o_ref, x_ref, cur_ref, old_ref, left_ref, right_ref):
    lane = lax.broadcasted_iota(jnp.int32, (SUB, LANES), 1)
    sub = lax.broadcasted_iota(jnp.int32, (SUB, LANES), 0)
    nb, n, _ = x_ref.shape
    mask = plan.mask()
    first = lax.axis_index("station") * plan.per
    row = lax.broadcasted_iota(jnp.int32, (n, n), 0)
    col = lax.broadcasted_iota(jnp.int32, (n, n), 1)
    for q in range(nb):
        prior = prior_ref[pl.ds(plan.block(q, mask) - first, 1), :]
        t = unpack(a_ref[q] + b_ref[q])
        x = t + t.T + jnp.where(row == col, jnp.broadcast_to(prior, (n, n)), 0.0)
        x_ref[q] = x
        cur_ref[q] = x[:PANEL]
        old_ref[q] = x[:PANEL]
    left_ref[...] = jnp.zeros_like(left_ref)
    right_ref[...] = jnp.zeros_like(right_ref)

    def update(q, prev):
        inside = (col >= prev) & (col < prev + PANEL)
        return jnp.where(inside, 0.0, x_ref[q]) - mxu(left_ref[q], right_ref[q], NN)

    def step(k, c):
        base = k * PANEL
        last = pl.ds(pl.multiple_of(jnp.maximum(base - PANEL, 0), PANEL), PANEL)
        after = pl.ds(pl.multiple_of(jnp.minimum(base + PANEL, n - PANEL), PANEL), PANEL)
        inside = (lane >= base) & (lane < base + PANEL)
        for q in range(nb):
            cur = cur_ref[q]
            rows = [jnp.broadcast_to(cur_ref[q, i:i + 1, :], (SUB, LANES)) for i in range(PANEL)]
            out = eliminate(rows, base, lane)
            x_ref[q] = update(q, base - PANEL)
            x_ref[q, last, :] = old_ref[q]
            y = x_ref[q, after, :]
            t = jnp.where(inside, 0.0, y)
            for j in range(PANEL - 1, -1, -1):
                t = t - pick(y, jnp.zeros((SUB, LANES), jnp.int32) + (base + j)) * out[j]
            cur_ref[q] = t
            panel = out[0]
            for i in range(1, PANEL):
                panel = jnp.where(sub == i, out[i], panel)
            old_ref[q] = panel
            left_ref[q] = left_of(jnp.where(lane < base, -cur, cur))
            right_ref[q] = right_of(panel)
        return c

    lax.fori_loop(0, n // PANEL, step, 0)
    for q in range(nb):
        o_ref[q] = pack(jnp.concatenate([update(q, n - PANEL)[:n - PANEL], old_ref[q]], 0))


def bias_kernel(plan, dims, vis_ref, near_ref, far_ref, sol_ref, cov_ref, part_ref, tab_ref, two_ref):
    stations, slots, n, width = dims
    half = near_ref.shape[0]
    for p in range(NHALF):
        x = unpack(near_ref[p] if p < half else far_ref[p - half])
        tab_ref[p] = x
        two_ref[p] = stacked(x, 1)
    mask = plan.mask()
    first = lax.axis_index("station") * plan.per
    for b in range(plan.per):
        x = tab_ref[plan.position(first + b, mask)]
        cov_ref[b] = x + x.T

    def one(s):
        hi, lo, lifted = [], [], []
        for j in range(slots):
            v = vis_ref[s, j]
            at = plan.position(jnp.minimum(v, NHALF - 1), mask)
            x = split(sol_ref[s, j] * jnp.where(v < NHALF, 1.0, 0.0))
            hi.append(x[0])
            lo.append(x[1])
            lifted.append(corner(mxu(jnp.concatenate(x, 0), two_ref[at], NN), n, width))
        right = jnp.concatenate([jnp.concatenate(hi, 1), jnp.concatenate(lo, 1)], 0)
        total = corner(mxu(stacked(jnp.concatenate(lifted, 1), 0), right, NT), n, n)
        return total + total.T

    pairs = stations // 2

    def pair(s, c):
        part_ref[pl.ds(pl.multiple_of(s * n, SUB), n), 0:n] = one(s)
        part_ref[pl.ds(pl.multiple_of(s * n, SUB), n), 64:64 + n] = one(s + pairs)
        return c

    lax.fori_loop(0, pairs, pair, 0)


def last_kernel(dims, len_ref, uni_ref, inv_ref, a_ref, b_ref, o_ref, map_ref, res_ref):
    stations, slots, n, width = dims
    for i in range(n):
        map_ref[pl.ds(i, stations, stride=n), :] = row_of(uni_ref, i, n).astype(f32)
    pairs = stations // 2
    r = lax.broadcasted_iota(jnp.int32, (n, n), 0)
    c = lax.broadcasted_iota(jnp.int32, (n, n), 1)
    for s in range(stations):
        keep = (r < len_ref[s]) & (c < len_ref[s])
        rows = slice((s % pairs) * n, (s % pairs) * n + n)
        cols = slice(0, n) if s < pairs else slice(64, 64 + n)
        part = a_ref[rows, cols] + b_ref[rows, cols]
        cov = jnp.where(keep, inv_ref[s * n:s * n + n, :n] + part, 0.0)
        z = map_ref[s * n:s * n + n, :n]
        zs = z.astype(bf16)
        hi, lo = split(cov)

        def d(x, y, dd):
            return lax.dot_general(x, y, (dd, ((), ())), preferred_element_type=f32)

        left = d(zs, hi, NN) + d(zs, lo, NN)
        hi, lo = split(left)
        res_ref[s * n:s * n + n, :n] = jnp.where(keep, d(hi, zs, NT) + d(lo, zs, NT), 0.0)
    for i in range(n):
        o_ref[:, i * n:i * n + n] = res_ref[pl.ds(i, stations, stride=n), :][:, :n]


def vmem():
    return pl.BlockSpec(memory_space=pltpu.VMEM)


def hbm():
    return pl.BlockSpec(memory_space=pltpu.HBM)


def smem():
    return pl.BlockSpec(memory_space=pltpu.SMEM)


def local(plan, normal_mat, coupling, lengths, visible, bias_prior, unimod):
    stations, _, slots, n, width = coupling.shape
    dims = (stations, slots, n, width)
    cpl = coupling.reshape(dims)
    vis = visible.reshape(stations, slots)
    sds = jax.ShapeDtypeStruct
    sizes = []
    size = NHALF
    for _ in plan.steps:
        size //= 2
        sizes.append(size)
    sizes.append(size)
    inv, sol, *parts = pl.pallas_call(
        functools.partial(first_kernel, plan, dims),
        out_shape=[sds((stations * n, LANES), f32), sds(dims, f32)] + [sds((q, width // 2 + SUB, width), f32) for q in sizes],
        in_specs=[hbm()] * 4,
        out_specs=[vmem()] * (2 + len(sizes)),
        scratch_shapes=[
            pltpu.SMEM(lengths.shape, jnp.int32),
            pltpu.SMEM(vis.shape, jnp.int32),
            pltpu.VMEM(normal_mat.shape, f32),
            pltpu.VMEM(dims, f32),
            pltpu.VMEM((stations * PANEL, LANES), f32),
            pltpu.VMEM((NHALF + 1, width, width), f32),
            pltpu.SemaphoreType.DMA((4,)),
        ],
        compiler_params=PARAMS,
    )(*(pltpu.with_memory_space_constraint(x, pltpu.HBM) for x in (lengths, vis, normal_mat, cpl)))

    got = None
    for t, (axis, bit, _) in enumerate(plan.steps):
        send = parts[t]
        if got is not None:
            size = send.shape[0]
            send, got = send + got[size:], got[:size]
        new = lax.ppermute(send, axis, plan.perm(axis, bit))
        got = new if got is None else got + new
    keep = parts[-1]
    for axis, bit in plan.sums:
        total = got + keep
        got = lax.ppermute(total, axis, plan.perm(axis, bit))
        keep = total
    cov = pl.pallas_call(
        functools.partial(invert_kernel, plan),
        out_shape=sds(keep.shape, f32),
        in_specs=[vmem()] * 3,
        out_specs=vmem(),
        scratch_shapes=[
            pltpu.VMEM((keep.shape[0], width, width), f32),
            pltpu.VMEM((keep.shape[0], PANEL, width), f32),
            pltpu.VMEM((keep.shape[0], PANEL, width), f32),
            pltpu.VMEM((keep.shape[0], width, 6 * PANEL), bf16),
            pltpu.VMEM((keep.shape[0], 6 * PANEL, width), bf16),
        ],
        compiler_params=PARAMS,
    )(bias_prior.reshape(bias_prior.shape[1:]), keep, got)
    near, far = cov, None
    for axis, bit, _ in reversed(plan.steps):
        if far is not None:
            near = jnp.concatenate([near, far], 0)
        far = lax.ppermute(near, axis, plan.perm(axis, bit))
    bias_cov, part = pl.pallas_call(
        functools.partial(bias_kernel, plan, dims),
        out_shape=[sds((plan.per, width, width), f32), sds((stations // 2 * n, LANES), f32)],
        in_specs=[smem()] + [vmem()] * 3,
        out_specs=[vmem()] * 2,
        scratch_shapes=[pltpu.VMEM((NHALF, width, width), f32), pltpu.VMEM((NHALF, width, 2 * width), bf16)],
        compiler_params=PARAMS,
    )(vis, near, far, sol)
    other = lax.ppermute(part, "bias", [(0, 1), (1, 0)])
    amb = pl.pallas_call(
        functools.partial(last_kernel, dims),
        out_shape=sds((stations, n * n), f32),
        in_specs=[smem()] + [vmem()] * 4,
        out_specs=vmem(),
        scratch_shapes=[pltpu.VMEM((stations * n, LANES), f32)] * 2,
        compiler_params=PARAMS,
    )(lengths, unimod, inv, part, other)
    return bias_cov.reshape((1,) + bias_cov.shape), amb


def solution(mesh):
    plan = Plan(mesh.shape["station"], mesh.shape["group"])
    return jax.shard_map(
        functools.partial(local, plan),
        mesh=mesh,
        in_specs=(
            P(("station", "group"), None),
            P(("station", "group"), "bias", None, None, None),
            P(("station", "group")),
            P(("station", "group"), "bias", None),
            P("bias", "station", None),
            P(("station", "group"), None),
        ),
        out_specs=(P("bias", "station", None, None), P(("station", "group"), None)),
        check_vma=False,
    )
```

```python
import functools

import jax
import jax.numpy as jnp
from jax import lax
from jax.experimental import pallas as pl
from jax.experimental.pallas import tpu as pltpu
from jax.sharding import PartitionSpec as P

NHALF = 16
LANES = 128
SUB = 8
PANEL = 8
f32 = jnp.float32
bf16 = jnp.bfloat16

PARAMS = pltpu.CompilerParams(vmem_limit_bytes=16 << 20)


def bits_of(n):
    count = n.bit_length() - 1
    assert 1 << count == n
    return count


class Plan:
    def __init__(self, stations, groups):
        per = max(NHALF // stations, 1)
        own = min(bits_of(per), bits_of(groups))
        steps = [("group", g, bits_of(per) - 1 - g) for g in range(own)]
        steps += [("station", z, bits_of(per) + z) for z in range(bits_of(stations))]
        self.per = per
        self.sizes = {"station": stations, "group": groups}
        self.steps = steps
        self.sums = [("group", g) for g in range(own, bits_of(groups))]
        used = [b for _, _, b in steps]
        rest = [b for b in range(bits_of(NHALF)) if b not in used]
        top = bits_of(NHALF) - 1
        self.moves = [(top - t, b) for t, b in enumerate(used)]
        self.moves += list(zip(range(len(rest)), sorted(rest)))
        self.left = NHALF >> len(steps)

    def mask(self):
        out = 0
        for axis, bit, block_bit in self.steps:
            out = out + (((lax.axis_index(axis) >> bit) & 1) << block_bit)
        return out

    def position(self, block, mask):
        y = block ^ mask
        out = 0
        for p, b in self.moves:
            out = out + (((y >> b) & 1) << p)
        return out

    def block(self, position, mask):
        out = 0
        for p, b in self.moves:
            out = out + (((position >> p) & 1) << b)
        return out ^ mask

    def perm(self, axis, bit):
        return [(i, i ^ (1 << bit)) for i in range(self.sizes[axis])]


def split(x):
    hi = x.astype(bf16)
    return hi, (x - hi.astype(f32)).astype(bf16)


def dot3(a, b, dims):
    def d(x, y):
        return lax.dot_general(x, y, (dims, ((), ())), preferred_element_type=f32)

    return d(a[0], b[0]) + (d(a[0], b[1]) + d(a[1], b[0]))


def split3(x):
    hi = x.astype(bf16).astype(f32)
    rest = x - hi
    mid = rest.astype(bf16).astype(f32)
    return hi, mid, rest - mid


def left_of(a, base):
    lane = lax.broadcasted_iota(jnp.int32, (SUB, LANES), 1)
    idx = base + (lane & (PANEL - 1))
    t = jnp.concatenate([pick(a[v:v + SUB], idx) for v in range(0, a.shape[0], SUB)], 0)
    hi, mid, lo = split3(t)
    group = lax.broadcasted_iota(jnp.int32, a.shape, 1) // PANEL
    t = jnp.where((group == 2) | (group == 5), mid, jnp.where(group == 4, lo, hi))
    return t.astype(bf16)[:, :6 * PANEL]


def turned(x):
    hi, mid, lo = split3(x)
    return jnp.concatenate([hi, hi, mid, hi, lo, mid], 0).T.astype(bf16)


def right_of(r):
    hi, mid, lo = split3(r)
    return jnp.concatenate([hi, mid, hi, lo, hi, mid], 0).astype(bf16)


NN = ((1,), (0,))
NT = ((1,), (1,))


def mxu(a, b, dims):
    return lax.dot_general(a, b, (dims, ((), ())), preferred_element_type=f32)


def stacked(x, axis):
    return jnp.concatenate(split(x), axis)


def identity(n):
    row = lax.broadcasted_iota(jnp.int32, (n, n), 0)
    return (row == lax.broadcasted_iota(jnp.int32, (n, n), 1)).astype(f32).astype(bf16)


def corner(y, m, n):
    return y[:m, :n] + (y[:m, n:] + y[m:, :n])


def pick(x, idx):
    return jnp.take_along_axis(x, idx, axis=1)


def eliminate(rows, base, lane):
    b = len(rows)
    idx = [jnp.zeros((SUB, LANES), jnp.int32) + (base + j) for j in range(b)]
    p = [[pick(rows[i], idx[j]) for j in range(i + 1)] for i in range(b)]
    inside = (lane >= base) & (lane < base + b)
    y = [jnp.where(inside, (lane == base + i).astype(f32), rows[i]) for i in range(b)]
    l = [[None] * b for _ in range(b)]
    r = [None] * b
    for j in range(b):
        r[j] = 1.0 / p[j][j]
        for i in range(j + 1, b):
            l[i][j] = p[i][j] * r[j]
        for i in range(j + 1, b):
            for m in range(j + 1, i + 1):
                p[i][m] = p[i][m] - l[i][j] * p[m][j]
        for i in range(j + 1, b):
            y[i] = y[i] - l[i][j] * y[j]
    out = [None] * b
    for i in range(b - 1, -1, -1):
        t = y[i] * r[i]
        for j in range(b - 1, i, -1):
            t = t - l[j][i] * out[j]
        out[i] = t
    return out


def tile_iota(n):
    row = lax.broadcasted_iota(jnp.int32, (n, 2 * n), 0)
    lane = lax.broadcasted_iota(jnp.int32, (n, 2 * n), 1)
    return row, lane


def pack(x):
    n = x.shape[0] // 2
    row, lane = tile_iota(n)
    top, low = x[:n], x[n:]
    body = jnp.where((lane >= n) | (row >= lane), top, pltpu.roll(low, n, 1))
    diag = jnp.where(row == lane - n, low, 0.0)
    tail = diag[:SUB]
    for v in range(1, n // SUB):
        tail = tail + diag[v * SUB:v * SUB + SUB]
    return jnp.concatenate([body, tail], 0)


def unpack(y):
    n = y.shape[1] // 2
    row, lane = tile_iota(n)
    body, tail = y[:n], y[n:]
    top = jnp.where((lane >= n) | (row > lane), body, jnp.where(row == lane, 0.5 * body, 0.0))
    spread = jnp.concatenate([tail] * (n // SUB), 0)
    low = jnp.where(lane - n > row, pltpu.roll(body, n, 1), jnp.where(row == lane - n, 0.5 * spread, 0.0))
    return jnp.concatenate([top, low], 0)


def row_of(ref, i, n):
    at = i * n
    tile, off = at // LANES, at % LANES
    x = ref[:, tile * LANES:(tile + 1) * LANES]
    if off:
        x = pltpu.roll(x, LANES - off, 1)
        if off + n > LANES:
            nxt = ref[:, (tile + 1) * LANES:(tile + 2) * LANES]
            nxt = pltpu.roll(nxt, LANES - off, 1)
            lane = lax.broadcasted_iota(jnp.int32, (SUB, LANES), 1)
            x = jnp.where(lane < LANES - off, x, nxt)
    return x


def lengths_column(len_ref, stations):
    sub = lax.broadcasted_iota(jnp.int32, (SUB, LANES), 0)
    out = jnp.zeros((SUB, LANES), jnp.int32)
    for s in range(stations):
        out = jnp.where(sub == s, len_ref[s], out)
    return out


def first_kernel(plan, dims, len_hbm, vis_hbm, mat_hbm, cpl_hbm, inv_ref, sol_ref, *rest):
    stations, slots, n, width = dims
    outs, (len_ref, vis_ref, mat_ref, cpl_ref, pad_ref, acc_ref, sem) = rest[:-7], rest[-7:]
    pairs = ((len_hbm, len_ref), (mat_hbm, mat_ref), (vis_hbm, vis_ref), (cpl_hbm, cpl_ref))
    loads = [pltpu.make_async_copy(src, dst, sem.at[t]) for t, (src, dst) in enumerate(pairs)]
    for load in loads:
        load.start()
    acc_ref[...] = jnp.zeros_like(acc_ref)
    loads[0].wait()
    loads[1].wait()
    lane = lax.broadcasted_iota(jnp.int32, (SUB, LANES), 1)
    length = lengths_column(len_ref, stations)
    for i in range(n):
        x = row_of(mat_ref, i, n)
        keep = (lane < length) & (length > i)
        inv_ref[pl.ds(i, stations, stride=n), :] = jnp.where(keep, x, (lane == i).astype(f32))
    wide = lax.broadcasted_iota(jnp.int32, (n, LANES), 1)

    def step(k, c):
        base = k * PANEL
        at = [pl.ds(base + i, stations, stride=n) for i in range(PANEL)]
        out = eliminate([inv_ref[at[i], :] for i in range(PANEL)], base, lane)
        for i in range(PANEL):
            pad_ref[pl.ds(i, stations, stride=PANEL), :] = out[i]
        inside = (wide >= base) & (wide < base + PANEL)
        for s in range(stations):
            rows = slice(s * n, s * n + n)
            a = inv_ref[rows, :]
            right = right_of(pad_ref[s * PANEL:s * PANEL + PANEL, :])
            inv_ref[rows, :] = jnp.where(inside, 0.0, a) - mxu(left_of(a, base), right, NN)
        for i in range(PANEL):
            inv_ref[at[i], :] = out[i]
        return c

    lax.fori_loop(0, n // PANEL, step, 0)
    loads[2].wait()
    loads[3].wait()
    mask = plan.mask()
    tall = lax.broadcasted_iota(jnp.int32, (n, width), 0)

    def station(s, c):
        inverse = stacked(inv_ref[pl.ds(pl.multiple_of(s * n, SUB), n), :n], 0)
        valid = tall < len_ref[s]
        ws, ds = [], []
        for j in range(slots):
            w = jnp.where(valid, cpl_ref[s, j], 0.0)
            hi, lo = split(w)
            x = corner(mxu(inverse, jnp.concatenate([hi, lo], 1), NN), n, width)
            sol_ref[s, j] = x
            ws.append(jnp.concatenate([hi, lo], 0).T)
            d = stacked(w - x, 1)
            ds.append(jnp.concatenate([d, d], 0))
        for j in range(slots):
            red = mxu(ws[j], ds[j], NN)
            v = vis_ref[s, j]
            at = jnp.where(v < NHALF, plan.position(v, mask), NHALF)
            acc_ref[at] += red[:, :width] + red[:, width:]
        return c

    lax.fori_loop(0, stations, station, 0)
    at = NHALF
    for o in outs:
        at -= o.shape[0]
        for q in range(o.shape[0]):
            o[q] = pack(acc_ref[at + q])


def invert_kernel(plan, prior_ref, a_ref, b_ref, o_ref, x_ref, cur_ref, old_ref, right_ref, left_ref):
    lane = lax.broadcasted_iota(jnp.int32, (SUB, LANES), 1)
    sub = lax.broadcasted_iota(jnp.int32, (SUB, LANES), 0)
    nb, n, _ = x_ref.shape
    mask = plan.mask()
    first = lax.axis_index("station") * plan.per
    row = lax.broadcasted_iota(jnp.int32, (n, n), 0)
    col = lax.broadcasted_iota(jnp.int32, (n, n), 1)
    for q in range(nb):
        prior = prior_ref[pl.ds(plan.block(q, mask) - first, 1), :]
        t = unpack(a_ref[q] + b_ref[q])
        x = t + t.T + jnp.where(row == col, jnp.broadcast_to(prior, (n, n)), 0.0)
        x_ref[q] = x
        cur_ref[q] = x[:PANEL]
        old_ref[q] = x[:PANEL]
    right_ref[...] = jnp.zeros_like(right_ref)
    left_ref[...] = jnp.zeros_like(left_ref)

    def update(q, prev):
        inside = (col >= prev) & (col < prev + PANEL)
        a = x_ref[q]
        return jnp.where(inside, 0.0, a) - mxu(left_ref[q], right_ref[q], NN)

    def step(k, c):
        base = k * PANEL
        last = pl.ds(pl.multiple_of(jnp.maximum(base - PANEL, 0), PANEL), PANEL)
        after = pl.ds(pl.multiple_of(jnp.minimum(base + PANEL, n - PANEL), PANEL), PANEL)
        inside = (lane >= base) & (lane < base + PANEL)
        every = range(nb)
        cols = [jnp.zeros((SUB, LANES), jnp.int32) + (base + j) for j in range(PANEL)]
        cur = [cur_ref[q] for q in every]
        rows = [[jnp.broadcast_to(cur_ref[q, i:i + 1, :], (SUB, LANES)) for i in range(PANEL)] for q in every]
        new = [update(q, base - PANEL) for q in every]
        out = [eliminate(rows[q], base, lane) for q in every]
        for q in every:
            x_ref[q] = new[q]
            x_ref[q, last, :] = old_ref[q]
            left_ref[q] = turned(jnp.where(lane < base, -cur[q], cur[q]))
        for q in every:
            y = x_ref[q, after, :]
            t = jnp.where(inside, 0.0, y)
            for j in range(PANEL - 1, -1, -1):
                t = t - pick(y, cols[j]) * out[q][j]
            cur[q] = t
        for q in every:
            panel = out[q][0]
            for i in range(1, PANEL):
                panel = jnp.where(sub == i, out[q][i], panel)
            cur_ref[q] = cur[q]
            old_ref[q] = panel
            right_ref[q] = right_of(panel)
        return c

    lax.fori_loop(0, n // PANEL, step, 0)
    for q in range(nb):
        o_ref[q] = pack(jnp.concatenate([update(q, n - PANEL)[:n - PANEL], old_ref[q]], 0))


def bias_kernel(plan, dims, vis_ref, near_ref, far_ref, sol_ref, part_ref, two_ref):
    stations, slots, n, width = dims
    half = near_ref.shape[0]
    for p in range(NHALF):
        x = unpack(near_ref[p] if p < half else far_ref[p - half])
        two_ref[p] = stacked(x, 1)
    mask = plan.mask()
    def one(s):
        hi, lo, lifted = [], [], []
        for j in range(slots):
            v = vis_ref[s, j]
            at = plan.position(jnp.minimum(v, NHALF - 1), mask)
            x = split(sol_ref[s, j] * jnp.where(v < NHALF, 1.0, 0.0))
            hi.append(x[0])
            lo.append(x[1])
            lifted.append(corner(mxu(jnp.concatenate(x, 0), two_ref[at], NN), n, width))
        right = jnp.concatenate([jnp.concatenate(hi, 1), jnp.concatenate(lo, 1)], 0)
        total = corner(mxu(stacked(jnp.concatenate(lifted, 1), 0), right, NT), n, n)
        return total + total.T

    pairs = stations // 2

    def pair(s, c):
        part_ref[pl.ds(pl.multiple_of(s * n, SUB), n), 0:n] = one(s)
        part_ref[pl.ds(pl.multiple_of(s * n, SUB), n), 64:64 + n] = one(s + pairs)
        return c

    lax.fori_loop(0, pairs, pair, 0)


def cov_kernel(plan, near_ref, far_ref, o_ref):
    half = near_ref.shape[0]
    mask = plan.mask()
    first = lax.axis_index("station") * plan.per
    for b in range(plan.per):
        p = plan.position(first + b, mask)
        y = jnp.where(p < half, near_ref[jnp.minimum(p, half - 1)], far_ref[jnp.maximum(p - half, 0)])
        x = unpack(y)
        o_ref[b] = x + x.T


def last_kernel(dims, len_ref, uni_ref, inv_ref, a_ref, b_ref, o_ref, map_ref, res_ref):
    stations, slots, n, width = dims
    for i in range(n):
        map_ref[pl.ds(i, stations, stride=n), :] = row_of(uni_ref, i, n).astype(f32)
    pairs = stations // 2
    r = lax.broadcasted_iota(jnp.int32, (n, n), 0)
    c = lax.broadcasted_iota(jnp.int32, (n, n), 1)
    for s in range(stations):
        keep = (r < len_ref[s]) & (c < len_ref[s])
        rows = slice((s % pairs) * n, (s % pairs) * n + n)
        cols = slice(0, n) if s < pairs else slice(64, 64 + n)
        part = a_ref[rows, cols] + b_ref[rows, cols]
        cov = jnp.where(keep, inv_ref[s * n:s * n + n, :n] + part, 0.0)
        z = map_ref[s * n:s * n + n, :n]
        zs = z.astype(bf16)
        hi, lo = split(cov)

        def d(x, y, dd):
            return lax.dot_general(x, y, (dd, ((), ())), preferred_element_type=f32)

        left = d(zs, hi, NN) + d(zs, lo, NN)
        hi, lo = split(left)
        res_ref[s * n:s * n + n, :n] = jnp.where(keep, d(hi, zs, NT) + d(lo, zs, NT), 0.0)
    for i in range(n):
        o_ref[:, i * n:i * n + n] = res_ref[pl.ds(i, stations, stride=n), :][:, :n]


def vmem():
    return pl.BlockSpec(memory_space=pltpu.VMEM)


def hbm():
    return pl.BlockSpec(memory_space=pltpu.HBM)


def smem():
    return pl.BlockSpec(memory_space=pltpu.SMEM)


def local(plan, normal_mat, coupling, lengths, visible, bias_prior, unimod):
    stations, _, slots, n, width = coupling.shape
    dims = (stations, slots, n, width)
    cpl = coupling.reshape(dims)
    vis = visible.reshape(stations, slots)
    sds = jax.ShapeDtypeStruct
    sizes = []
    size = NHALF
    for _ in plan.steps:
        size //= 2
        sizes.append(size)
    sizes.append(size)
    inv, sol, *parts = pl.pallas_call(
        functools.partial(first_kernel, plan, dims),
        out_shape=[sds((stations * n, LANES), f32), sds(dims, f32)] + [sds((q, width // 2 + SUB, width), f32) for q in sizes],
        in_specs=[hbm()] * 4,
        out_specs=[vmem()] * (2 + len(sizes)),
        scratch_shapes=[
            pltpu.SMEM(lengths.shape, jnp.int32),
            pltpu.SMEM(vis.shape, jnp.int32),
            pltpu.VMEM(normal_mat.shape, f32),
            pltpu.VMEM(dims, f32),
            pltpu.VMEM((stations * PANEL, LANES), f32),
            pltpu.VMEM((NHALF + 1, width, width), f32),
            pltpu.SemaphoreType.DMA((4,)),
        ],
        compiler_params=PARAMS,
    )(*(pltpu.with_memory_space_constraint(x, pltpu.HBM) for x in (lengths, vis, normal_mat, cpl)))

    got = None
    for t, (axis, bit, _) in enumerate(plan.steps):
        send = parts[t]
        if got is not None:
            size = send.shape[0]
            send, got = send + got[size:], got[:size]
        new = lax.ppermute(send, axis, plan.perm(axis, bit))
        got = new if got is None else got + new
    keep = parts[-1]
    for axis, bit in plan.sums:
        total = got + keep
        got = lax.ppermute(total, axis, plan.perm(axis, bit))
        keep = total
    cov = pl.pallas_call(
        functools.partial(invert_kernel, plan),
        out_shape=sds(keep.shape, f32),
        in_specs=[vmem()] * 3,
        out_specs=vmem(),
        scratch_shapes=[
            pltpu.VMEM((keep.shape[0], width, width), f32),
            pltpu.VMEM((keep.shape[0], PANEL, width), f32),
            pltpu.VMEM((keep.shape[0], PANEL, width), f32),
            pltpu.VMEM((keep.shape[0], 6 * PANEL, width), bf16),
            pltpu.VMEM((keep.shape[0], width, 6 * PANEL), bf16),
        ],
        compiler_params=PARAMS,
    )(bias_prior.reshape(bias_prior.shape[1:]), keep, got)
    near, far = cov, None
    for axis, bit, _ in reversed(plan.steps):
        if far is not None:
            near = jnp.concatenate([near, far], 0)
        far = lax.ppermute(near, axis, plan.perm(axis, bit))
    part = pl.pallas_call(
        functools.partial(bias_kernel, plan, dims),
        out_shape=sds((stations // 2 * n, LANES), f32),
        in_specs=[smem()] + [vmem()] * 3,
        out_specs=vmem(),
        scratch_shapes=[pltpu.VMEM((NHALF, width, 2 * width), bf16)],
        compiler_params=PARAMS,
    )(vis, near, far, sol)
    other = lax.ppermute(part, "bias", [(0, 1), (1, 0)])
    bias_cov = pl.pallas_call(
        functools.partial(cov_kernel, plan),
        out_shape=sds((plan.per, width, width), f32),
        in_specs=[vmem()] * 2,
        out_specs=vmem(),
        compiler_params=PARAMS,
        cost_estimate=pl.CostEstimate(flops=1 << 20, bytes_accessed=4 << 20, transcendentals=0),
    )(near, far)
    amb = pl.pallas_call(
        functools.partial(last_kernel, dims),
        out_shape=sds((stations, n * n), f32),
        in_specs=[smem()] + [vmem()] * 4,
        out_specs=vmem(),
        scratch_shapes=[pltpu.VMEM((stations * n, LANES), f32)] * 2,
        compiler_params=PARAMS,
    )(lengths, unimod, inv, part, other)
    return bias_cov.reshape((1,) + bias_cov.shape), amb


def solution(mesh):
    plan = Plan(mesh.shape["station"], mesh.shape["group"])
    return jax.shard_map(
        functools.partial(local, plan),
        mesh=mesh,
        in_specs=(
            P(("station", "group"), None),
            P(("station", "group"), "bias", None, None, None),
            P(("station", "group")),
            P(("station", "group"), "bias", None),
            P("bias", "station", None),
            P(("station", "group"), None),
        ),
        out_specs=(P("bias", "station", None, None), P(("station", "group"), None)),
        check_vma=False,
    )
```

```python
import functools

import jax
import jax.numpy as jnp
from jax import lax
from jax.experimental import pallas as pl
from jax.experimental.pallas import tpu as pltpu
from jax.sharding import PartitionSpec as P

NHALF = 16
LANES = 128
SUB = 8
PANEL = 8
f32 = jnp.float32
bf16 = jnp.bfloat16

PARAMS = pltpu.CompilerParams(vmem_limit_bytes=16 << 20)


def bits_of(n):
    count = n.bit_length() - 1
    assert 1 << count == n
    return count


class Plan:
    def __init__(self, stations, groups):
        per = max(NHALF // stations, 1)
        own = min(bits_of(per), bits_of(groups))
        stages = [("group", [(g, bits_of(per) - 1 - g)]) for g in range(own)]
        z = [(b, bits_of(per) + b) for b in range(bits_of(stations))]
        stages += [("station", z[i:i + 2]) for i in range(0, len(z), 2)]
        self.per = per
        self.sizes = {"station": stations, "group": groups}
        self.stages = stages
        self.sums = [("group", g) for g in range(own, bits_of(groups))]
        used = [b for _, bits in stages for _, b in bits]
        rest = [b for b in range(bits_of(NHALF)) if b not in used]
        top = bits_of(NHALF) - 1
        self.moves = [(top - t, b) for t, b in enumerate(used)]
        self.moves += list(zip(range(len(rest)), sorted(rest)))

    def mask(self):
        out = 0
        for axis, bits in self.stages:
            for bit, block_bit in bits:
                out = out + (((lax.axis_index(axis) >> bit) & 1) << block_bit)
        return out

    def position(self, block, mask):
        y = block ^ mask
        out = 0
        for p, b in self.moves:
            out = out + (((y >> b) & 1) << p)
        return out

    def block(self, position, mask):
        out = 0
        for p, b in self.moves:
            out = out + (((position >> p) & 1) << b)
        return out ^ mask

    def perm(self, axis, bit):
        return [(i, i ^ (1 << bit)) for i in range(self.sizes[axis])]

    def partners(self, stage):
        axis, bits = stage
        out = []
        for d in range(1, 1 << len(bits)):
            flip = 0
            for i, (bit, _) in enumerate(reversed(bits)):
                flip |= ((d >> i) & 1) << bit
            out.append((d, [(i, i ^ flip) for i in range(self.sizes[axis])]))
        return out


def split(x):
    hi = x.astype(bf16)
    return hi, (x - hi.astype(f32)).astype(bf16)


def dot3(a, b, dims):
    def d(x, y):
        return lax.dot_general(x, y, (dims, ((), ())), preferred_element_type=f32)

    return d(a[0], b[0]) + (d(a[0], b[1]) + d(a[1], b[0]))


def split3(x):
    hi = x.astype(bf16).astype(f32)
    rest = x - hi
    mid = rest.astype(bf16).astype(f32)
    return hi, mid, rest - mid


def left_of(a, base):
    lane = lax.broadcasted_iota(jnp.int32, (SUB, LANES), 1)
    idx = base + (lane & (PANEL - 1))
    t = jnp.concatenate([pick(a[v:v + SUB], idx) for v in range(0, a.shape[0], SUB)], 0)
    hi, mid, lo = split3(t)
    group = lax.broadcasted_iota(jnp.int32, a.shape, 1) // PANEL
    t = jnp.where((group == 2) | (group == 5), mid, jnp.where(group == 4, lo, hi))
    return t.astype(bf16)[:, :6 * PANEL]


def turned(x):
    hi, mid, lo = split3(x)
    return jnp.concatenate([hi, hi, mid, hi, lo, mid], 0).T.astype(bf16)


def right_of(r):
    hi, mid, lo = split3(r)
    return jnp.concatenate([hi, mid, hi, lo, hi, mid], 0).astype(bf16)


NN = ((1,), (0,))
NT = ((1,), (1,))


def mxu(a, b, dims):
    return lax.dot_general(a, b, (dims, ((), ())), preferred_element_type=f32)


def stacked(x, axis):
    return jnp.concatenate(split(x), axis)


def identity(n):
    row = lax.broadcasted_iota(jnp.int32, (n, n), 0)
    return (row == lax.broadcasted_iota(jnp.int32, (n, n), 1)).astype(f32).astype(bf16)


def corner(y, m, n):
    return y[:m, :n] + (y[:m, n:] + y[m:, :n])


def pick(x, idx):
    return jnp.take_along_axis(x, idx, axis=1)


def eliminate(rows, base, lane):
    b = len(rows)
    idx = [jnp.zeros((SUB, LANES), jnp.int32) + (base + j) for j in range(b)]
    p = [[pick(rows[i], idx[j]) for j in range(i + 1)] for i in range(b)]
    inside = (lane >= base) & (lane < base + b)
    y = [jnp.where(inside, (lane == base + i).astype(f32), rows[i]) for i in range(b)]
    l = [[None] * b for _ in range(b)]
    r = [None] * b
    for j in range(b):
        r[j] = 1.0 / p[j][j]
        for i in range(j + 1, b):
            l[i][j] = p[i][j] * r[j]
        for i in range(j + 1, b):
            for m in range(j + 1, i + 1):
                p[i][m] = p[i][m] - l[i][j] * p[m][j]
        for i in range(j + 1, b):
            y[i] = y[i] - l[i][j] * y[j]
    out = [None] * b
    for i in range(b - 1, -1, -1):
        t = y[i] * r[i]
        for j in range(b - 1, i, -1):
            t = t - l[j][i] * out[j]
        out[i] = t
    return out


def tile_iota(n):
    row = lax.broadcasted_iota(jnp.int32, (n, 2 * n), 0)
    lane = lax.broadcasted_iota(jnp.int32, (n, 2 * n), 1)
    return row, lane


def pack(x):
    n = x.shape[0] // 2
    row, lane = tile_iota(n)
    top, low = x[:n], x[n:]
    body = jnp.where((lane >= n) | (row >= lane), top, pltpu.roll(low, n, 1))
    diag = jnp.where(row == lane - n, low, 0.0)
    tail = diag[:SUB]
    for v in range(1, n // SUB):
        tail = tail + diag[v * SUB:v * SUB + SUB]
    return jnp.concatenate([body, tail], 0)


def unpack(y):
    n = y.shape[1] // 2
    row, lane = tile_iota(n)
    body, tail = y[:n], y[n:]
    top = jnp.where((lane >= n) | (row > lane), body, jnp.where(row == lane, 0.5 * body, 0.0))
    spread = jnp.concatenate([tail] * (n // SUB), 0)
    low = jnp.where(lane - n > row, pltpu.roll(body, n, 1), jnp.where(row == lane - n, 0.5 * spread, 0.0))
    return jnp.concatenate([top, low], 0)


def row_of(ref, i, n):
    at = i * n
    tile, off = at // LANES, at % LANES
    x = ref[:, tile * LANES:(tile + 1) * LANES]
    if off:
        x = pltpu.roll(x, LANES - off, 1)
        if off + n > LANES:
            nxt = ref[:, (tile + 1) * LANES:(tile + 2) * LANES]
            nxt = pltpu.roll(nxt, LANES - off, 1)
            lane = lax.broadcasted_iota(jnp.int32, (SUB, LANES), 1)
            x = jnp.where(lane < LANES - off, x, nxt)
    return x


def lengths_column(len_ref, stations):
    sub = lax.broadcasted_iota(jnp.int32, (SUB, LANES), 0)
    out = jnp.zeros((SUB, LANES), jnp.int32)
    for s in range(stations):
        out = jnp.where(sub == s, len_ref[s], out)
    return out


def first_kernel(plan, dims, len_hbm, vis_hbm, mat_hbm, cpl_hbm, inv_ref, sol_ref, *rest):
    stations, slots, n, width = dims
    outs, (len_ref, vis_ref, mat_ref, cpl_ref, pad_ref, acc_ref, sem) = rest[:-7], rest[-7:]
    pairs = ((len_hbm, len_ref), (mat_hbm, mat_ref), (vis_hbm, vis_ref), (cpl_hbm, cpl_ref))
    loads = [pltpu.make_async_copy(src, dst, sem.at[t]) for t, (src, dst) in enumerate(pairs)]
    for load in loads:
        load.start()
    acc_ref[...] = jnp.zeros_like(acc_ref)
    loads[0].wait()
    loads[1].wait()
    lane = lax.broadcasted_iota(jnp.int32, (SUB, LANES), 1)
    length = lengths_column(len_ref, stations)
    for i in range(n):
        x = row_of(mat_ref, i, n)
        keep = (lane < length) & (length > i)
        inv_ref[pl.ds(i, stations, stride=n), :] = jnp.where(keep, x, (lane == i).astype(f32))
    wide = lax.broadcasted_iota(jnp.int32, (n, LANES), 1)

    def step(k, c):
        base = k * PANEL
        at = [pl.ds(base + i, stations, stride=n) for i in range(PANEL)]
        out = eliminate([inv_ref[at[i], :] for i in range(PANEL)], base, lane)
        for i in range(PANEL):
            pad_ref[pl.ds(i, stations, stride=PANEL), :] = out[i]
        inside = (wide >= base) & (wide < base + PANEL)
        for s in range(stations):
            rows = slice(s * n, s * n + n)
            a = inv_ref[rows, :]
            right = right_of(pad_ref[s * PANEL:s * PANEL + PANEL, :])
            inv_ref[rows, :] = jnp.where(inside, 0.0, a) - mxu(left_of(a, base), right, NN)
        for i in range(PANEL):
            inv_ref[at[i], :] = out[i]
        return c

    lax.fori_loop(0, n // PANEL, step, 0)
    loads[2].wait()
    loads[3].wait()
    mask = plan.mask()
    tall = lax.broadcasted_iota(jnp.int32, (n, width), 0)

    def station(s, c):
        inverse = stacked(inv_ref[pl.ds(pl.multiple_of(s * n, SUB), n), :n], 0)
        valid = tall < len_ref[s]
        ws, ds = [], []
        for j in range(slots):
            w = jnp.where(valid, cpl_ref[s, j], 0.0)
            hi, lo = split(w)
            x = corner(mxu(inverse, jnp.concatenate([hi, lo], 1), NN), n, width)
            sol_ref[s, j] = x
            ws.append(jnp.concatenate([hi, lo], 0).T)
            d = stacked(w - x, 1)
            ds.append(jnp.concatenate([d, d], 0))
        for j in range(slots):
            red = mxu(ws[j], ds[j], NN)
            v = vis_ref[s, j]
            at = jnp.where(v < NHALF, plan.position(v, mask), NHALF)
            acc_ref[at] += red[:, :width] + red[:, width:]
        return c

    lax.fori_loop(0, stations, station, 0)
    at = NHALF
    for o in outs:
        at -= o.shape[0]
        for q in range(o.shape[0]):
            o[q] = pack(acc_ref[at + q])


def invert_kernel(plan, prior_ref, a_ref, b_ref, o_ref, x_ref, cur_ref, old_ref, right_ref, left_ref):
    lane = lax.broadcasted_iota(jnp.int32, (SUB, LANES), 1)
    sub = lax.broadcasted_iota(jnp.int32, (SUB, LANES), 0)
    nb, n, _ = x_ref.shape
    mask = plan.mask()
    first = lax.axis_index("station") * plan.per
    row = lax.broadcasted_iota(jnp.int32, (n, n), 0)
    col = lax.broadcasted_iota(jnp.int32, (n, n), 1)
    for q in range(nb):
        prior = prior_ref[pl.ds(plan.block(q, mask) - first, 1), :]
        t = unpack(a_ref[q] + b_ref[q])
        x = t + t.T + jnp.where(row == col, jnp.broadcast_to(prior, (n, n)), 0.0)
        x_ref[q] = x
        cur_ref[q] = x[:PANEL]
        old_ref[q] = x[:PANEL]
    right_ref[...] = jnp.zeros_like(right_ref)
    left_ref[...] = jnp.zeros_like(left_ref)

    def update(q, prev):
        inside = (col >= prev) & (col < prev + PANEL)
        a = x_ref[q]
        return jnp.where(inside, 0.0, a) - mxu(left_ref[q], right_ref[q], NN)

    def step(k, c):
        base = k * PANEL
        last = pl.ds(pl.multiple_of(jnp.maximum(base - PANEL, 0), PANEL), PANEL)
        after = pl.ds(pl.multiple_of(jnp.minimum(base + PANEL, n - PANEL), PANEL), PANEL)
        inside = (lane >= base) & (lane < base + PANEL)
        every = range(nb)
        cols = [jnp.zeros((SUB, LANES), jnp.int32) + (base + j) for j in range(PANEL)]
        cur = [cur_ref[q] for q in every]
        rows = [[jnp.broadcast_to(cur_ref[q, i:i + 1, :], (SUB, LANES)) for i in range(PANEL)] for q in every]
        new = [update(q, base - PANEL) for q in every]
        out = [eliminate(rows[q], base, lane) for q in every]
        for q in every:
            x_ref[q] = new[q]
            x_ref[q, last, :] = old_ref[q]
            left_ref[q] = turned(jnp.where(lane < base, -cur[q], cur[q]))
        for q in every:
            y = x_ref[q, after, :]
            t = jnp.where(inside, 0.0, y)
            for j in range(PANEL - 1, -1, -1):
                t = t - pick(y, cols[j]) * out[q][j]
            cur[q] = t
        for q in every:
            panel = out[q][0]
            for i in range(1, PANEL):
                panel = jnp.where(sub == i, out[q][i], panel)
            cur_ref[q] = cur[q]
            old_ref[q] = panel
            right_ref[q] = right_of(panel)
        return c

    lax.fori_loop(0, n // PANEL, step, 0)
    for q in range(nb):
        o_ref[q] = pack(jnp.concatenate([update(q, n - PANEL)[:n - PANEL], old_ref[q]], 0))


def bias_kernel(plan, dims, vis_ref, near_ref, far_ref, sol_ref, part_ref, two_ref):
    stations, slots, n, width = dims
    half = near_ref.shape[0]
    for p in range(NHALF):
        x = unpack(near_ref[p] if p < half else far_ref[p - half])
        two_ref[p] = stacked(x, 1)
    mask = plan.mask()
    def one(s):
        hi, lo, lifted = [], [], []
        for j in range(slots):
            v = vis_ref[s, j]
            at = plan.position(jnp.minimum(v, NHALF - 1), mask)
            x = split(sol_ref[s, j] * jnp.where(v < NHALF, 1.0, 0.0))
            hi.append(x[0])
            lo.append(x[1])
            lifted.append(corner(mxu(jnp.concatenate(x, 0), two_ref[at], NN), n, width))
        right = jnp.concatenate([jnp.concatenate(hi, 1), jnp.concatenate(lo, 1)], 0)
        total = corner(mxu(stacked(jnp.concatenate(lifted, 1), 0), right, NT), n, n)
        return total + total.T

    for s in range(stations):
        part_ref[:, s * n:s * n + n] = one(s)


def cov_kernel(plan, near_ref, far_ref, o_ref):
    half = near_ref.shape[0]
    mask = plan.mask()
    first = lax.axis_index("station") * plan.per
    for b in range(plan.per):
        p = plan.position(first + b, mask)
        y = jnp.where(p < half, near_ref[jnp.minimum(p, half - 1)], far_ref[jnp.maximum(p - half, 0)])
        x = unpack(y)
        o_ref[b] = x + x.T


def map_kernel(dims, uni_ref, map_ref):
    stations, _, n, _ = dims
    for i in range(n):
        map_ref[pl.ds(i, stations, stride=n), :] = row_of(uni_ref, i, n).astype(f32)


def last_kernel(dims, len_ref, map_ref, inv_ref, a_ref, b_ref, o_ref, res_ref):
    stations, slots, n, width = dims
    r = lax.broadcasted_iota(jnp.int32, (n, n), 0)
    c = lax.broadcasted_iota(jnp.int32, (n, n), 1)
    for s in range(stations):
        keep = (r < len_ref[s]) & (c < len_ref[s])
        at = slice(s * n, s * n + n)
        part = a_ref[:, at] + b_ref[:, at]
        cov = jnp.where(keep, inv_ref[s * n:s * n + n, :n] + part, 0.0)
        z = map_ref[s * n:s * n + n, :n]
        zs = z.astype(bf16)
        hi, lo = split(cov)

        def d(x, y, dd):
            return lax.dot_general(x, y, (dd, ((), ())), preferred_element_type=f32)

        left = d(zs, hi, NN) + d(zs, lo, NN)
        hi, lo = split(left)
        res_ref[s * n:s * n + n, :n] = jnp.where(keep, d(hi, zs, NT) + d(lo, zs, NT), 0.0)
    for i in range(n):
        o_ref[:, i * n:i * n + n] = res_ref[pl.ds(i, stations, stride=n), :][:, :n]


def vmem():
    return pl.BlockSpec(memory_space=pltpu.VMEM)


def hbm():
    return pl.BlockSpec(memory_space=pltpu.HBM)


def smem():
    return pl.BlockSpec(memory_space=pltpu.SMEM)


def local(plan, normal_mat, coupling, lengths, visible, bias_prior, unimod):
    stations, _, slots, n, width = coupling.shape
    dims = (stations, slots, n, width)
    cpl = coupling.reshape(dims)
    vis = visible.reshape(stations, slots)
    sds = jax.ShapeDtypeStruct
    sizes = []
    size = NHALF
    for _, bits in plan.stages:
        size >>= len(bits)
        sizes += [size] * ((1 << len(bits)) - 1)
    sizes.append(size)
    inv, sol, *parts = pl.pallas_call(
        functools.partial(first_kernel, plan, dims),
        out_shape=[sds((stations * n, LANES), f32), sds(dims, f32)] + [sds((q, width // 2 + SUB, width), f32) for q in sizes],
        in_specs=[hbm()] * 4,
        out_specs=[vmem()] * (2 + len(sizes)),
        scratch_shapes=[
            pltpu.SMEM(lengths.shape, jnp.int32),
            pltpu.SMEM(vis.shape, jnp.int32),
            pltpu.VMEM(normal_mat.shape, f32),
            pltpu.VMEM(dims, f32),
            pltpu.VMEM((stations * PANEL, LANES), f32),
            pltpu.VMEM((NHALF + 1, width, width), f32),
            pltpu.SemaphoreType.DMA((4,)),
        ],
        compiler_params=PARAMS,
    )(*(pltpu.with_memory_space_constraint(x, pltpu.HBM) for x in (lengths, vis, normal_mat, cpl)))

    got, at = None, 0
    for stage in plan.stages:
        new = None
        partners = plan.partners(stage)
        for d, perm in reversed(partners):
            send = parts[at]
            at += 1
            size = send.shape[0]
            if got is not None:
                send = send + got[d * size:d * size + size]
            arrived = lax.ppermute(send, stage[0], perm)
            new = arrived if new is None else new + arrived
        got = new if got is None else got[:size] + new
    keep = parts[-1]
    for axis, bit in plan.sums:
        total = got + keep
        got = lax.ppermute(total, axis, plan.perm(axis, bit))
        keep = total
    cov = pl.pallas_call(
        functools.partial(invert_kernel, plan),
        out_shape=sds(keep.shape, f32),
        in_specs=[vmem()] * 3,
        out_specs=vmem(),
        scratch_shapes=[
            pltpu.VMEM((keep.shape[0], width, width), f32),
            pltpu.VMEM((keep.shape[0], PANEL, width), f32),
            pltpu.VMEM((keep.shape[0], PANEL, width), f32),
            pltpu.VMEM((keep.shape[0], 6 * PANEL, width), bf16),
            pltpu.VMEM((keep.shape[0], width, 6 * PANEL), bf16),
        ],
        compiler_params=PARAMS,
    )(bias_prior.reshape(bias_prior.shape[1:]), keep, got)
    near, far = cov, []
    for stage in reversed(plan.stages):
        near = jnp.concatenate([near] + far, 0)
        far = [lax.ppermute(near, stage[0], perm) for _, perm in plan.partners(stage)]
    far = jnp.concatenate(far, 0)
    part = pl.pallas_call(
        functools.partial(bias_kernel, plan, dims),
        out_shape=sds((n, stations * n), f32),
        in_specs=[smem()] + [vmem()] * 3,
        out_specs=vmem(),
        scratch_shapes=[pltpu.VMEM((NHALF, width, 2 * width), bf16)],
        compiler_params=PARAMS,
    )(vis, near, far, sol)
    other = lax.ppermute(part, "bias", [(0, 1), (1, 0)])
    bias_cov = pl.pallas_call(
        functools.partial(cov_kernel, plan),
        out_shape=sds((plan.per, width, width), f32),
        in_specs=[vmem()] * 2,
        out_specs=vmem(),
        compiler_params=PARAMS,
        cost_estimate=pl.CostEstimate(flops=1 << 20, bytes_accessed=4 << 20, transcendentals=0),
    )(near, far)
    maps = pl.pallas_call(
        functools.partial(map_kernel, dims),
        out_shape=sds((stations * n, LANES), f32),
        in_specs=[vmem()],
        out_specs=vmem(),
        compiler_params=PARAMS,
        cost_estimate=pl.CostEstimate(flops=1 << 20, bytes_accessed=2 << 20, transcendentals=0),
    )(unimod)
    amb = pl.pallas_call(
        functools.partial(last_kernel, dims),
        out_shape=sds((stations, n * n), f32),
        in_specs=[smem()] + [vmem()] * 4,
        out_specs=vmem(),
        scratch_shapes=[pltpu.VMEM((stations * n, LANES), f32)],
        compiler_params=PARAMS,
    )(lengths, maps, inv, part, other)
    return bias_cov.reshape((1,) + bias_cov.shape), amb


def solution(mesh):
    plan = Plan(mesh.shape["station"], mesh.shape["group"])
    return jax.shard_map(
        functools.partial(local, plan),
        mesh=mesh,
        in_specs=(
            P(("station", "group"), None),
            P(("station", "group"), "bias", None, None, None),
            P(("station", "group")),
            P(("station", "group"), "bias", None),
            P("bias", "station", None),
            P(("station", "group"), None),
        ),
        out_specs=(P("bias", "station", None, None), P(("station", "group"), None)),
        check_vma=False,
    )
```

```python
import functools

import jax
import jax.numpy as jnp
from jax import lax
from jax.experimental import pallas as pl
from jax.experimental.pallas import tpu as pltpu
from jax.sharding import PartitionSpec as P

NHALF = 16
LANES = 128
SUB = 8
PANEL = 8
f32 = jnp.float32
bf16 = jnp.bfloat16

PARAMS = pltpu.CompilerParams(vmem_limit_bytes=16 << 20)


def bits_of(n):
    count = n.bit_length() - 1
    assert 1 << count == n
    return count


class Plan:
    def __init__(self, stations, groups):
        per = max(NHALF // stations, 1)
        own = min(bits_of(per), bits_of(groups))
        stages = [("group", [(g, bits_of(per) - 1 - g)]) for g in range(own)]
        z = [(b, bits_of(per) + b) for b in range(bits_of(stations))]
        stages += [("station", z[i:i + 2]) for i in range(0, len(z), 2)]
        self.per = per
        self.sizes = {"station": stations, "group": groups}
        self.stages = stages
        self.sums = [("group", g) for g in range(own, bits_of(groups))]
        used = [b for _, bits in stages for _, b in bits]
        rest = [b for b in range(bits_of(NHALF)) if b not in used]
        top = bits_of(NHALF) - 1
        self.moves = [(top - t, b) for t, b in enumerate(used)]
        self.moves += list(zip(range(len(rest)), sorted(rest)))

    def mask(self):
        out = 0
        for axis, bits in self.stages:
            for bit, block_bit in bits:
                out = out + (((lax.axis_index(axis) >> bit) & 1) << block_bit)
        return out

    def position(self, block, mask):
        y = block ^ mask
        out = 0
        for p, b in self.moves:
            out = out + (((y >> b) & 1) << p)
        return out

    def block(self, position, mask):
        out = 0
        for p, b in self.moves:
            out = out + (((position >> p) & 1) << b)
        return out ^ mask

    def perm(self, axis, bit):
        return [(i, i ^ (1 << bit)) for i in range(self.sizes[axis])]

    def partners(self, stage):
        axis, bits = stage
        out = []
        for d in range(1, 1 << len(bits)):
            flip = 0
            for i, (bit, _) in enumerate(reversed(bits)):
                flip |= ((d >> i) & 1) << bit
            out.append((d, [(i, i ^ flip) for i in range(self.sizes[axis])]))
        return out


def split(x):
    hi = x.astype(bf16)
    return hi, (x - hi.astype(f32)).astype(bf16)


def dot3(a, b, dims):
    def d(x, y):
        return lax.dot_general(x, y, (dims, ((), ())), preferred_element_type=f32)

    return d(a[0], b[0]) + (d(a[0], b[1]) + d(a[1], b[0]))


def split3(x):
    hi = x.astype(bf16).astype(f32)
    rest = x - hi
    mid = rest.astype(bf16).astype(f32)
    return hi, mid, rest - mid


def left_of(a, base):
    lane = lax.broadcasted_iota(jnp.int32, (SUB, LANES), 1)
    idx = base + (lane & (PANEL - 1))
    t = jnp.concatenate([pick(a[v:v + SUB], idx) for v in range(0, a.shape[0], SUB)], 0)
    hi, mid, lo = split3(t)
    group = lax.broadcasted_iota(jnp.int32, a.shape, 1) // PANEL
    t = jnp.where((group == 2) | (group == 5), mid, jnp.where(group == 4, lo, hi))
    return t.astype(bf16)[:, :6 * PANEL]


def turned(x):
    hi, mid, lo = split3(x)
    return jnp.concatenate([hi, hi, mid, hi, lo, mid], 0).T.astype(bf16)


def right_of(r):
    hi, mid, lo = split3(r)
    return jnp.concatenate([hi, mid, hi, lo, hi, mid], 0).astype(bf16)


NN = ((1,), (0,))
NT = ((1,), (1,))


def mxu(a, b, dims):
    return lax.dot_general(a, b, (dims, ((), ())), preferred_element_type=f32)


def stacked(x, axis):
    return jnp.concatenate(split(x), axis)


def identity(n):
    row = lax.broadcasted_iota(jnp.int32, (n, n), 0)
    return (row == lax.broadcasted_iota(jnp.int32, (n, n), 1)).astype(f32).astype(bf16)


def corner(y, m, n):
    return y[:m, :n] + (y[:m, n:] + y[m:, :n])


def pick(x, idx):
    return jnp.take_along_axis(x, idx, axis=1)


def eliminate(rows, base, lane):
    b = len(rows)
    idx = [jnp.zeros((SUB, LANES), jnp.int32) + (base + j) for j in range(b)]
    p = [[pick(rows[i], idx[j]) for j in range(i + 1)] for i in range(b)]
    inside = (lane >= base) & (lane < base + b)
    y = [jnp.where(inside, (lane == base + i).astype(f32), rows[i]) for i in range(b)]
    l = [[None] * b for _ in range(b)]
    r = [None] * b
    for j in range(b):
        r[j] = 1.0 / p[j][j]
        for i in range(j + 1, b):
            l[i][j] = p[i][j] * r[j]
        for i in range(j + 1, b):
            for m in range(j + 1, i + 1):
                p[i][m] = p[i][m] - l[i][j] * p[m][j]
        for i in range(j + 1, b):
            y[i] = y[i] - l[i][j] * y[j]
    out = [None] * b
    for i in range(b - 1, -1, -1):
        t = y[i] * r[i]
        for j in range(b - 1, i, -1):
            t = t - l[j][i] * out[j]
        out[i] = t
    return out


def tile_iota(n):
    row = lax.broadcasted_iota(jnp.int32, (n, 2 * n), 0)
    lane = lax.broadcasted_iota(jnp.int32, (n, 2 * n), 1)
    return row, lane


def pack(x):
    n = x.shape[0] // 2
    row, lane = tile_iota(n)
    top, low = x[:n], x[n:]
    body = jnp.where((lane >= n) | (row >= lane), top, pltpu.roll(low, n, 1))
    diag = jnp.where(row == lane - n, low, 0.0)
    tail = diag[:SUB]
    for v in range(1, n // SUB):
        tail = tail + diag[v * SUB:v * SUB + SUB]
    return jnp.concatenate([body, tail], 0)


def unpack(y):
    n = y.shape[1] // 2
    row, lane = tile_iota(n)
    body, tail = y[:n], y[n:]
    top = jnp.where((lane >= n) | (row > lane), body, jnp.where(row == lane, 0.5 * body, 0.0))
    spread = jnp.concatenate([tail] * (n // SUB), 0)
    low = jnp.where(lane - n > row, pltpu.roll(body, n, 1), jnp.where(row == lane - n, 0.5 * spread, 0.0))
    return jnp.concatenate([top, low], 0)


def row_of(ref, i, n):
    at = i * n
    tile, off = at // LANES, at % LANES
    x = ref[:, tile * LANES:(tile + 1) * LANES]
    if off:
        x = pltpu.roll(x, LANES - off, 1)
        if off + n > LANES:
            nxt = ref[:, (tile + 1) * LANES:(tile + 2) * LANES]
            nxt = pltpu.roll(nxt, LANES - off, 1)
            lane = lax.broadcasted_iota(jnp.int32, (SUB, LANES), 1)
            x = jnp.where(lane < LANES - off, x, nxt)
    return x


def lengths_column(len_ref, stations):
    sub = lax.broadcasted_iota(jnp.int32, (SUB, LANES), 0)
    out = jnp.zeros((SUB, LANES), jnp.int32)
    for s in range(stations):
        out = jnp.where(sub == s, len_ref[s], out)
    return out


def first_kernel(plan, dims, len_hbm, vis_hbm, mat_hbm, cpl_hbm, inv_ref, sol_ref, *rest):
    stations, slots, n, width = dims
    outs, (len_ref, vis_ref, mat_ref, cpl_ref, pad_ref, acc_ref, sem) = rest[:-7], rest[-7:]
    pairs = ((len_hbm, len_ref), (mat_hbm, mat_ref), (vis_hbm, vis_ref), (cpl_hbm, cpl_ref))
    loads = [pltpu.make_async_copy(src, dst, sem.at[t]) for t, (src, dst) in enumerate(pairs)]
    for load in loads:
        load.start()
    acc_ref[...] = jnp.zeros_like(acc_ref)
    loads[0].wait()
    loads[1].wait()
    lane = lax.broadcasted_iota(jnp.int32, (SUB, LANES), 1)
    length = lengths_column(len_ref, stations)
    for i in range(n):
        x = row_of(mat_ref, i, n)
        keep = (lane < length) & (length > i)
        inv_ref[pl.ds(i, stations, stride=n), :] = jnp.where(keep, x, (lane == i).astype(f32))
    wide = lax.broadcasted_iota(jnp.int32, (n, LANES), 1)

    def step(k, c):
        base = k * PANEL
        at = [pl.ds(base + i, stations, stride=n) for i in range(PANEL)]
        out = eliminate([inv_ref[at[i], :] for i in range(PANEL)], base, lane)
        for i in range(PANEL):
            pad_ref[pl.ds(i, stations, stride=PANEL), :] = out[i]
        inside = (wide >= base) & (wide < base + PANEL)
        for s in range(stations):
            rows = slice(s * n, s * n + n)
            a = inv_ref[rows, :]
            right = right_of(pad_ref[s * PANEL:s * PANEL + PANEL, :])
            inv_ref[rows, :] = jnp.where(inside, 0.0, a) - mxu(left_of(a, base), right, NN)
        for i in range(PANEL):
            inv_ref[at[i], :] = out[i]
        return c

    for k in range(n // PANEL):
        step(k, 0)
    loads[2].wait()
    loads[3].wait()
    mask = plan.mask()
    tall = lax.broadcasted_iota(jnp.int32, (n, width), 0)

    def station(s, c):
        inverse = stacked(inv_ref[s * n:s * n + n, :n], 0)
        valid = tall < len_ref[s]
        ws, ds = [], []
        for j in range(slots):
            w = jnp.where(valid, cpl_ref[s, j], 0.0)
            hi, lo = split(w)
            x = corner(mxu(inverse, jnp.concatenate([hi, lo], 1), NN), n, width)
            sol_ref[s, j] = x
            ws.append(jnp.concatenate([hi, lo], 0).T)
            d = stacked(w - x, 1)
            ds.append(jnp.concatenate([d, d], 0))
        for j in range(slots):
            red = mxu(ws[j], ds[j], NN)
            v = vis_ref[s, j]
            at = jnp.where(v < NHALF, plan.position(v, mask), NHALF)
            acc_ref[at] += red[:, :width] + red[:, width:]
        return c

    for s in range(stations):
        station(s, 0)
    at = NHALF
    for o in outs:
        at -= o.shape[0]
        for q in range(o.shape[0]):
            o[q] = pack(acc_ref[at + q])


def invert_kernel(plan, prior_ref, a_ref, b_ref, o_ref, x_ref, cur_ref, next_ref, old_ref, right_ref, left_ref):
    lane = lax.broadcasted_iota(jnp.int32, (SUB, LANES), 1)
    sub = lax.broadcasted_iota(jnp.int32, (SUB, LANES), 0)
    nb, n, _ = x_ref.shape
    mask = plan.mask()
    first = lax.axis_index("station") * plan.per
    row = lax.broadcasted_iota(jnp.int32, (n, n), 0)
    col = lax.broadcasted_iota(jnp.int32, (n, n), 1)
    for q in range(nb):
        prior = prior_ref[pl.ds(plan.block(q, mask) - first, 1), :]
        t = unpack(a_ref[q] + b_ref[q])
        x = t + t.T + jnp.where(row == col, jnp.broadcast_to(prior, (n, n)), 0.0)
        x_ref[q] = x
        cur_ref[q] = x[:PANEL]
        old_ref[q] = x[:PANEL]
        next_ref[q] = x[PANEL:2 * PANEL]
    right_ref[...] = jnp.zeros_like(right_ref)
    left_ref[...] = jnp.zeros_like(left_ref)

    def update(q, prev):
        inside = (col >= prev) & (col < prev + PANEL)
        a = x_ref[q]
        return jnp.where(inside, 0.0, a) - mxu(left_ref[q], right_ref[q], NN)

    def step(k, c):
        base = k * PANEL
        last = pl.ds(max(base - PANEL, 0), PANEL)
        after = pl.ds(min(base + 2 * PANEL, n - PANEL), PANEL)
        inside = (lane >= base) & (lane < base + PANEL)
        every = range(nb)
        cols = [jnp.zeros((SUB, LANES), jnp.int32) + (base + j) for j in range(PANEL)]
        cur = [cur_ref[q] for q in every]
        rows = [[jnp.broadcast_to(cur_ref[q, i:i + 1, :], (SUB, LANES)) for i in range(PANEL)] for q in every]
        new = [update(q, base - PANEL) for q in every]
        out = [eliminate(rows[q], base, lane) for q in every]
        for q in every:
            x_ref[q] = new[q]
            x_ref[q, last, :] = old_ref[q]
            left_ref[q] = turned(jnp.where(lane < base, -cur[q], cur[q]))
        for q in every:
            for ref, y in ((cur_ref, next_ref[q]), (next_ref, x_ref[q, after, :])):
                t = jnp.where(inside, 0.0, y)
                for j in range(PANEL - 1, -1, -1):
                    t = t - pick(y, cols[j]) * out[q][j]
                ref[q] = t
        for q in every:
            panel = out[q][0]
            for i in range(1, PANEL):
                panel = jnp.where(sub == i, out[q][i], panel)
            old_ref[q] = panel
            right_ref[q] = right_of(panel)
        return c

    for k in range(n // PANEL):
        step(k, 0)
    for q in range(nb):
        o_ref[q] = pack(jnp.concatenate([update(q, n - PANEL)[:n - PANEL], old_ref[q]], 0))


def bias_kernel(plan, dims, vis_ref, near_ref, far_ref, sol_ref, part_ref, two_ref):
    stations, slots, n, width = dims
    half = near_ref.shape[0]
    for p in range(NHALF):
        x = unpack(near_ref[p] if p < half else far_ref[p - half])
        two_ref[p] = stacked(x, 1)
    mask = plan.mask()
    def one(s):
        hi, lo, lifted = [], [], []
        for j in range(slots):
            v = vis_ref[s, j]
            at = plan.position(jnp.minimum(v, NHALF - 1), mask)
            x = split(sol_ref[s, j] * jnp.where(v < NHALF, 1.0, 0.0))
            hi.append(x[0])
            lo.append(x[1])
            lifted.append(corner(mxu(jnp.concatenate(x, 0), two_ref[at], NN), n, width))
        right = jnp.concatenate([jnp.concatenate(hi, 1), jnp.concatenate(lo, 1)], 0)
        total = corner(mxu(stacked(jnp.concatenate(lifted, 1), 0), right, NT), n, n)
        return total + total.T

    for s in range(stations):
        part_ref[:, s * n:s * n + n] = one(s)


def cov_kernel(plan, near_ref, far_ref, o_ref):
    half = near_ref.shape[0]
    mask = plan.mask()
    first = lax.axis_index("station") * plan.per
    for b in range(plan.per):
        p = plan.position(first + b, mask)
        y = jnp.where(p < half, near_ref[jnp.minimum(p, half - 1)], far_ref[jnp.maximum(p - half, 0)])
        x = unpack(y)
        o_ref[b] = x + x.T


def map_kernel(dims, uni_ref, map_ref):
    stations, _, n, _ = dims
    lane = lax.broadcasted_iota(jnp.int32, (SUB, LANES), 1)
    for i in range(n):
        x = row_of(uni_ref, i, n).astype(f32)
        map_ref[pl.ds(i, stations, stride=n), :] = jnp.where(lane < n, x, pltpu.roll(x, n, 1))


def last_kernel(dims, len_ref, map_ref, inv_ref, a_ref, b_ref, o_ref, res_ref):
    stations, slots, n, width = dims
    r = lax.broadcasted_iota(jnp.int32, (n, n), 0)
    c = lax.broadcasted_iota(jnp.int32, (n, n), 1)
    keeps, maps, right = [], [], []
    for s in range(stations):
        keep = (r < len_ref[s]) & (c < len_ref[s])
        at = slice(s * n, s * n + n)
        cov = jnp.where(keep, inv_ref[at, :n] + (a_ref[:, at] + b_ref[:, at]), 0.0)
        z = map_ref[at, :2 * n].astype(bf16)
        y = mxu(stacked(cov, 0), z[:, :n], NT)
        keeps.append(keep)
        maps.append(z)
        right.append(stacked(y[:n] + y[n:], 0))
    for s in range(stations):
        res_ref[s * n:s * n + n, :n] = jnp.where(keeps[s], mxu(maps[s], right[s], NN), 0.0)
    for i in range(n):
        o_ref[:, i * n:i * n + n] = res_ref[pl.ds(i, stations, stride=n), :][:, :n]


def vmem():
    return pl.BlockSpec(memory_space=pltpu.VMEM)


def hbm():
    return pl.BlockSpec(memory_space=pltpu.HBM)


def smem():
    return pl.BlockSpec(memory_space=pltpu.SMEM)


def local(plan, normal_mat, coupling, lengths, visible, bias_prior, unimod):
    stations, _, slots, n, width = coupling.shape
    dims = (stations, slots, n, width)
    cpl = coupling.reshape(dims)
    vis = visible.reshape(stations, slots)
    sds = jax.ShapeDtypeStruct
    sizes = []
    size = NHALF
    for _, bits in plan.stages:
        size >>= len(bits)
        sizes += [size] * ((1 << len(bits)) - 1)
    sizes.append(size)
    inv, sol, *parts = pl.pallas_call(
        functools.partial(first_kernel, plan, dims),
        out_shape=[sds((stations * n, LANES), f32), sds(dims, f32)] + [sds((q, width // 2 + SUB, width), f32) for q in sizes],
        in_specs=[hbm()] * 4,
        out_specs=[vmem()] * (2 + len(sizes)),
        scratch_shapes=[
            pltpu.SMEM(lengths.shape, jnp.int32),
            pltpu.SMEM(vis.shape, jnp.int32),
            pltpu.VMEM(normal_mat.shape, f32),
            pltpu.VMEM(dims, f32),
            pltpu.VMEM((stations * PANEL, LANES), f32),
            pltpu.VMEM((NHALF + 1, width, width), f32),
            pltpu.SemaphoreType.DMA((4,)),
        ],
        compiler_params=PARAMS,
    )(*(pltpu.with_memory_space_constraint(x, pltpu.HBM) for x in (lengths, vis, normal_mat, cpl)))

    got, at = None, 0
    for stage in plan.stages:
        new = None
        partners = plan.partners(stage)
        for d, perm in reversed(partners):
            send = parts[at]
            at += 1
            size = send.shape[0]
            if got is not None:
                send = send + got[d * size:d * size + size]
            arrived = lax.ppermute(send, stage[0], perm)
            new = arrived if new is None else new + arrived
        got = new if got is None else got[:size] + new
    keep = parts[-1]
    for axis, bit in plan.sums:
        total = got + keep
        got = lax.ppermute(total, axis, plan.perm(axis, bit))
        keep = total
    cov = pl.pallas_call(
        functools.partial(invert_kernel, plan),
        out_shape=sds(keep.shape, f32),
        in_specs=[vmem()] * 3,
        out_specs=vmem(),
        scratch_shapes=[
            pltpu.VMEM((keep.shape[0], width, width), f32),
            pltpu.VMEM((keep.shape[0], PANEL, width), f32),
            pltpu.VMEM((keep.shape[0], PANEL, width), f32),
            pltpu.VMEM((keep.shape[0], PANEL, width), f32),
            pltpu.VMEM((keep.shape[0], 6 * PANEL, width), bf16),
            pltpu.VMEM((keep.shape[0], width, 6 * PANEL), bf16),
        ],
        compiler_params=PARAMS,
    )(bias_prior.reshape(bias_prior.shape[1:]), keep, got)
    near, far = cov, []
    for stage in reversed(plan.stages):
        near = jnp.concatenate([near] + far, 0)
        far = [lax.ppermute(near, stage[0], perm) for _, perm in plan.partners(stage)]
    far = jnp.concatenate(far, 0)
    part = pl.pallas_call(
        functools.partial(bias_kernel, plan, dims),
        out_shape=sds((n, stations * n), f32),
        in_specs=[smem()] + [vmem()] * 3,
        out_specs=vmem(),
        scratch_shapes=[pltpu.VMEM((NHALF, width, 2 * width), bf16)],
        compiler_params=PARAMS,
    )(vis, near, far, sol)
    other = lax.ppermute(part, "bias", [(0, 1), (1, 0)])
    bias_cov = pl.pallas_call(
        functools.partial(cov_kernel, plan),
        out_shape=sds((plan.per, width, width), f32),
        in_specs=[vmem()] * 2,
        out_specs=vmem(),
        compiler_params=PARAMS,
        cost_estimate=pl.CostEstimate(flops=1 << 20, bytes_accessed=4 << 20, transcendentals=0),
    )(near, far)
    maps = pl.pallas_call(
        functools.partial(map_kernel, dims),
        out_shape=sds((stations * n, LANES), f32),
        in_specs=[vmem()],
        out_specs=vmem(),
        compiler_params=PARAMS,
        cost_estimate=pl.CostEstimate(flops=1 << 20, bytes_accessed=2 << 20, transcendentals=0),
    )(unimod)
    amb = pl.pallas_call(
        functools.partial(last_kernel, dims),
        out_shape=sds((stations, n * n), f32),
        in_specs=[smem()] + [vmem()] * 4,
        out_specs=vmem(),
        scratch_shapes=[pltpu.VMEM((stations * n, LANES), f32)],
        compiler_params=PARAMS,
    )(lengths, maps, inv, part, other)
    return bias_cov.reshape((1,) + bias_cov.shape), amb


def solution(mesh):
    plan = Plan(mesh.shape["station"], mesh.shape["group"])
    return jax.shard_map(
        functools.partial(local, plan),
        mesh=mesh,
        in_specs=(
            P(("station", "group"), None),
            P(("station", "group"), "bias", None, None, None),
            P(("station", "group")),
            P(("station", "group"), "bias", None),
            P("bias", "station", None),
            P(("station", "group"), None),
        ),
        out_specs=(P("bias", "station", None, None), P(("station", "group"), None)),
        check_vma=False,
    )
```
